32 devices in a mesh: section: 2 (over y), expert: 16 (over z, x, core).
Axes of the slice: x: 2, y: 2, z: 4, core: 2. Of those that a mesh axis runs over, the one named last changes fastest.
Arguments:
- x_forward: bfloat16 [2, 1024, 2048], P('section', 'expert'), may hold values from -6 to 6
- norm_gain: float32 [2, 2048], P('section'), may hold values from 0.1 to 1.9
- w_gate: bfloat16 [2, 16, 2048, 768], P('section', 'expert'), may hold values from -0.125 to 0.125
- w_up: bfloat16 [2, 16, 2048, 768], P('section', 'expert'), may hold values from -0.125 to 0.125
- w_down: bfloat16 [2, 16, 768, 2048], P('section', 'expert'), may hold values from -0.21875 to 0.21875
- ids_forward: int32 [2, 1024, 8], P('section', 'expert'), may hold values from 0 to 15, all different within a row; in each aligned block of 64 rows (0 to 63, 64 to 127, ..., all dimensions but the last counted through in order) at most 48 rows name the same one
- gates_forward: float32 [2, 1024, 8], P('section', 'expert'), may hold values from 0.02 to 0.4
- x_backward: bfloat16 [2, 1024, 2048], P('section', 'expert'), may hold values from -6 to 6
- dy_backward: bfloat16 [2, 1024, 2048], P('section', 'expert'), may hold values from -6 to 6
- ids_backward: int32 [2, 1024, 8], P('section', 'expert'), may hold values from 0 to 15, all different within a row; in each aligned block of 64 rows (0 to 63, 64 to 127, ..., all dimensions but the last counted through in order) at most 48 rows name the same one
- gates_backward: float32 [2, 1024, 8], P('section', 'expert'), may hold values from 0.02 to 0.4
- saved_gate: bfloat16 [2, 16, 16, 48, 768], P('section', 'expert'), may hold values from -6 to 6
- saved_up: bfloat16 [2, 16, 16, 48, 768], P('section', 'expert'), may hold values from -6 to 6
Outputs:
- next_forward: bfloat16 [2, 1024, 2048], P('section', 'expert')
- next_backward: bfloat16 [2, 1024, 2048], P('section', 'expert')
The draws below stay inside these ranges and needn't reach their ends.
Inputs may be any that keep to these rules, and one draw needn't show every extreme that they name: `ids_forward`: each row names 8 different experts. In each aligned block of 64 tokens no expert is named by more than 48 tokens, a bound that some block reaches. `ids_backward`: each row names 8 different experts. In each aligned block of 64 tokens no expert is named by more than 48 tokens, a bound that some block reaches.
All inputs are finite; a program needn't handle non-finite values.
Results may differ from the reference program's by a relative error of at most 0.0043.
Values may be sent and summed in bfloat16 or wider, within the bound.
No kernel may reach another device: no remote copies, remote signals or barrier semaphores. Data moves between devices by JAX's collectives and lax.ppermute only.
A program may use at most 64 MiB of HBM per device.

```python
import math
import jax
import jax.numpy as jnp
import numpy as np
from jax import lax

D = 2048
FF = 768
TOP = 8
TOK_DEV = 64
SECTIONS = 2
EXPERTS = 16
BLOCKS = 16
TOKENS = 1024
CAP = 48


def steps_of(rng, shape, split, least, largest):
    def one(dim, blocks):
        draws = jax.random.uniform(jax.random.fold_in(jax.random.fold_in(rng, 6), dim), (blocks,), jnp.float32, least / len(split), largest / len(split))
        return jnp.repeat(jnp.exp(draws), shape[dim] // blocks).reshape((-1,) + (1,) * (len(shape) - dim - 1))

    level = one(*split[0])
    for cut in split[1:]:
        level = level * one(*cut)
    return level


def routed_block(rng, own, number, rows, amount, top, most, slope):
    order = jax.random.permutation(rng, amount)
    heavy_load, common = load_shares(amount, rows * top, most, slope, True), load_shares(amount, rows * top, most, slope, False)
    places = jnp.arange(amount)

    def named(lengths, turn):
        used = int((lengths > 0).sum())
        fixed = max(1, used // 4)
        passed = fixed + (places - fixed + turn * (used - fixed)) % max(1, amount - fixed)
        return jnp.zeros((amount,), jnp.int32).at[order[jnp.where(places < fixed, places, passed)]].set(jnp.asarray(lengths, jnp.int32))

    lengths = jnp.where(number % 4 == 0, named(heavy_load, number // 4), named(common, number - number // 4 - 1))
    mixed = jax.random.permutation(jax.random.fold_in(own, 3), amount)
    source_of, receiver = mixed[0:amount // 2 * 2:2], mixed[1:amount // 2 * 2:2]
    slack = jnp.minimum(lengths[source_of] - 1, most - lengths[receiver]) // 2
    slack = jnp.where((source_of == order[0]) | (receiver == order[0]) | (lengths[receiver] == 0), 0, jnp.maximum(slack, 0))
    passed = jax.random.randint(jax.random.fold_in(own, 4), (amount // 2,), 0, 1 << 20) % (slack + 1)
    lengths = lengths.at[source_of].add(-passed).at[receiver].add(passed)
    members = jnp.searchsorted(jnp.cumsum(lengths), jnp.arange(rows * top), side="right").astype(jnp.int32)
    listing = members.reshape(top, rows).T
    listing = listing[jax.random.permutation(jax.random.fold_in(own, 1), rows)]
    turn = jax.random.randint(jax.random.fold_in(own, 2), (rows, 1), 0, top)
    return jnp.take_along_axis(listing, (jnp.arange(top)[None, :] + turn) % top, axis=1)


def load_shares(number_of, total, most, slope, full):
    weights = [(1 << 20) // math.isqrt(rank ** slope) + 1 for rank in range(1, number_of + 1)]
    largest = most if full else min(most, max(-(-total // number_of), total * weights[0] // sum(weights)))
    least = 1 if total - largest >= number_of - 1 else 0
    counts, rest = [largest] + [least] * (number_of - 1), total - largest - least * (number_of - 1)
    while rest > 0:
        movable = [i for i in range(1, number_of) if counts[i] < largest] or [i for i in range(1, number_of) if counts[i] < most]
        mass, remaining = sum([weights[i] for i in movable]), rest
        for i in movable:
            addition = min(most - counts[i], max(1, remaining * weights[i] // mass), rest)
            counts[i] = counts[i] + addition
            rest = rest - addition
    return np.array(counts)


def normal_values(own_key, shape, width, reach, pieces=(), held_as=jnp.bfloat16):
    entries = width * jax.random.normal(own_key, shape, jnp.float32)
    if pieces:
        entries = entries * steps_of(own_key, shape, pieces, -0.22, 0.18)
    return jnp.clip(entries, -reach, reach).astype(held_as)


def setup_inputs(seed: int = 0) -> dict:
    streams_of = jax.random.split(jax.random.key(seed), 14)
    x_forward = normal_values(streams_of[0], (SECTIONS, TOKENS, D), 1.0, 6.0, ((0, 2), (1, 16)))
    norm_gain = jnp.clip(1.0 + 0.18 * jax.random.normal(streams_of[1], (SECTIONS, D), jnp.float32), 0.1, 1.9)
    w_gate = normal_values(streams_of[2], (SECTIONS, EXPERTS, D, FF), D ** -0.5, 0.125, ((0, 2), (1, 16)))
    w_up = normal_values(streams_of[3], (SECTIONS, EXPERTS, D, FF), D ** -0.5, 0.125, ((0, 2), (1, 16)))
    w_down = normal_values(streams_of[4], (SECTIONS, EXPERTS, FF, D), FF ** -0.5, 0.21875, ((0, 2), (1, 16)))
    ids_forward_keys = jax.random.split(jax.random.fold_in(streams_of[5], 1), SECTIONS * TOKENS // TOK_DEV)
    ids_forward_turns = jax.random.permutation(jax.random.fold_in(streams_of[5], 3), SECTIONS * TOKENS // TOK_DEV)
    ids_forward = jax.vmap(lambda own, number: routed_block(jax.random.fold_in(streams_of[5], 2), own, number, TOK_DEV, EXPERTS, TOP, CAP, 2))(ids_forward_keys, ids_forward_turns).reshape((SECTIONS, TOKENS, TOP))
    gates_forward = jnp.clip(0.02 + 0.38 * jax.random.uniform(streams_of[6], (SECTIONS, TOKENS, TOP), jnp.float32) ** steps_of(streams_of[6], (SECTIONS, TOKENS, TOP), ((0, 2), (1, 16)), -0.2, 0.2), 0.02, 0.4)
    x_backward = normal_values(streams_of[7], (SECTIONS, TOKENS, D), 1.0, 6.0, ((0, 2), (1, 16)))
    dy_backward = normal_values(streams_of[8], (SECTIONS, TOKENS, D), 1.0, 6.0, ((0, 2), (1, 16)))
    ids_backward_keys = jax.random.split(jax.random.fold_in(streams_of[9], 1), SECTIONS * TOKENS // TOK_DEV)
    ids_backward_turns = jax.random.permutation(jax.random.fold_in(streams_of[9], 3), SECTIONS * TOKENS // TOK_DEV)
    ids_backward = jax.vmap(lambda own, number: routed_block(jax.random.fold_in(streams_of[9], 2), own, number, TOK_DEV, EXPERTS, TOP, CAP, 2))(ids_backward_keys, ids_backward_turns).reshape((SECTIONS, TOKENS, TOP))
    gates_backward = jnp.clip(0.02 + 0.38 * jax.random.uniform(streams_of[10], (SECTIONS, TOKENS, TOP), jnp.float32) ** steps_of(streams_of[10], (SECTIONS, TOKENS, TOP), ((0, 2), (1, 16)), -0.2, 0.2), 0.02, 0.4)
    saved_gate = normal_values(streams_of[11], (SECTIONS, EXPERTS, BLOCKS, CAP, FF), 1.0, 6.0, ((0, 2), (1, 16)))
    saved_up = normal_values(streams_of[12], (SECTIONS, EXPERTS, BLOCKS, CAP, FF), 1.0, 6.0, ((0, 2), (1, 16)))
    return {"x_forward": x_forward, "norm_gain": norm_gain, "w_gate": w_gate, "w_up": w_up, "w_down": w_down, "ids_forward": ids_forward, "gates_forward": gates_forward, "x_backward": x_backward, "dy_backward": dy_backward, "ids_backward": ids_backward, "gates_backward": gates_backward, "saved_gate": saved_gate, "saved_up": saved_up}


epsilon = 1e-06

def slot_places(route_ids):
    flattened = route_ids.reshape(BLOCKS, TOK_DEV * TOP)
    onehot = (flattened[:, :, None] == jnp.arange(EXPERTS, dtype=jnp.int32)[None, None, :]).astype(jnp.int32)
    before = jnp.cumsum(onehot, axis=1) - onehot
    slot_index = lax.optimization_barrier(jnp.sum(before * onehot, axis=2)).astype(jnp.int32)
    block_ids = jnp.arange(BLOCKS, dtype=jnp.int32)[:, None]
    places = (flattened * BLOCKS + block_ids) * CAP + slot_index
    return places.reshape(TOKENS * TOP).astype(jnp.int32)

def dispatch_rows(rows, places):
    token_rows = (jnp.arange(TOKENS * TOP, dtype=jnp.int32) // TOP).astype(jnp.int32)
    buffer = jnp.zeros((EXPERTS * BLOCKS * CAP, D), rows.dtype)
    buffer = buffer.at[places].set(rows[token_rows])
    return buffer.reshape(EXPERTS, BLOCKS * CAP, D)

def combine_rows(results, places, weights):
    picked = results.reshape(EXPERTS * BLOCKS * CAP, D)[places].reshape(TOKENS, TOP, D)
    return lax.optimization_barrier(jnp.sum(weights[:, :, None] * picked.astype(jnp.float32), axis=1))

def inverse_rms(values):
    widened = values.astype(jnp.float32)
    return lax.rsqrt(lax.optimization_barrier(jnp.mean(widened * widened, axis=-1, keepdims=True)) + epsilon)

def expert_forward(inputs):
    rows, gate_matrix, up_matrix, down_matrix = inputs
    gate_pre = jnp.dot(rows, gate_matrix, preferred_element_type=jnp.float32)
    up_pre = jnp.dot(rows, up_matrix, preferred_element_type=jnp.float32)
    act_rows = (jax.nn.silu(gate_pre) * up_pre).astype(jnp.bfloat16)
    return jnp.dot(act_rows, down_matrix, preferred_element_type=jnp.float32).astype(jnp.bfloat16)

def expert_backward(inputs):
    grad_rows, gate_saved, up_saved, gate_matrix, up_matrix, down_matrix = inputs
    d_act = jnp.dot(grad_rows, down_matrix.T, preferred_element_type=jnp.float32)
    gate_pre = gate_saved.astype(jnp.float32)
    up_pre = up_saved.astype(jnp.float32)
    sigmoid_gate = jax.nn.sigmoid(gate_pre)
    d_gate = (d_act * up_pre * sigmoid_gate * (1.0 + gate_pre * (1.0 - sigmoid_gate))).astype(jnp.bfloat16)
    d_up = (d_act * gate_pre * sigmoid_gate).astype(jnp.bfloat16)
    summed = jnp.dot(d_gate, gate_matrix.T, preferred_element_type=jnp.float32)
    summed = summed + jnp.dot(d_up, up_matrix.T, preferred_element_type=jnp.float32)
    return summed.astype(jnp.bfloat16)

def one_section(inputs):
    x_forward, layer_gain, w_gate, w_up, w_down, ids_forward, gates_forward, x_backward, dy_backward, ids_backward, gates_backward, saved_gate, saved_up = inputs
    normed = (x_forward.astype(jnp.float32) * inverse_rms(x_forward) * layer_gain[None, :]).astype(jnp.bfloat16)
    places_forward = slot_places(ids_forward)
    rows_forward = dispatch_rows(normed, places_forward)
    expert_out = lax.map(expert_forward, (rows_forward, w_gate, w_up, w_down))
    layer_out = (x_forward.astype(jnp.float32) + combine_rows(expert_out, places_forward, gates_forward)).astype(jnp.bfloat16)
    places_backward = slot_places(ids_backward)
    rows_backward = dispatch_rows(dy_backward, places_backward)
    gate_keep = saved_gate.reshape(EXPERTS, BLOCKS * CAP, FF)
    up_keep = saved_up.reshape(EXPERTS, BLOCKS * CAP, FF)
    d_rows = lax.map(expert_backward, (rows_backward, gate_keep, up_keep, w_gate, w_up, w_down))
    d_normed = combine_rows(d_rows, places_backward, gates_backward)
    saved_input = x_backward.astype(jnp.float32)
    scale_rows = inverse_rms(x_backward)
    weighted = d_normed * layer_gain[None, :]
    inner = lax.optimization_barrier(jnp.mean(weighted * saved_input, axis=-1, keepdims=True))
    d_input = dy_backward.astype(jnp.float32) + scale_rows * weighted - saved_input * scale_rows * scale_rows * scale_rows * inner
    return (layer_out, d_input.astype(jnp.bfloat16))

def reference(x_forward, norm_gain, w_gate, w_up, w_down, ids_forward, gates_forward, x_backward, dy_backward, ids_backward, gates_backward, saved_gate, saved_up):
    layer_out, d_input = lax.map(one_section, (x_forward, norm_gain, w_gate, w_up, w_down, ids_forward, gates_forward, x_backward, dy_backward, ids_backward, gates_backward, saved_gate, saved_up))
    next_forward = jnp.roll(layer_out, 1, axis=0)
    next_backward = jnp.roll(d_input, -1, axis=0)
    return (next_forward, next_backward)
```

```python
import functools

import jax
import jax.numpy as jnp
from jax import lax
from jax.experimental import pallas as pl
from jax.experimental.pallas import tpu as pltpu
from jax.sharding import PartitionSpec as P

epsilon = 1e-06
f32 = jnp.float32
bf16 = jnp.bfloat16
LANES = 128
TILE = 256
TURNED = (((1,), (1,)), ((), ()))


def inverse_rms(values):
    widened = values.astype(f32)
    return lax.rsqrt(jnp.mean(widened * widened, axis=-1, keepdims=True) + epsilon)


def gate_columns(ids, gates, experts):
    onehot = ids[:, :, None] == jnp.arange(experts, dtype=jnp.int32)[None, None, :]
    dense = jnp.sum(jnp.where(onehot, gates[:, :, None], 0.0), axis=1)
    high = lax.reduce_precision(dense, 8, 7)
    low = dense - high
    both = jnp.concatenate([high, low], axis=1).astype(bf16)
    padded = -(-both.shape[1] // LANES) * LANES
    return jnp.pad(both, ((0, 0), (0, padded - both.shape[1])))


def experts_kernel(backward, experts, tokens, capacity, count, steps, scalars, *refs):
    rows, refs = refs[:count], refs[count:]
    mine, theirs, refs = refs[:3], refs[3:6], refs[6:]
    kept_mine, kept_theirs = (), ()
    if backward:
        kept_mine, kept_theirs, refs = refs[: 2 * count], refs[2 * count : 4 * count], refs[4 * count :]
    outs, refs = refs[:count], refs[count:]
    (gathered, total, gate_of), refs = refs[:3], refs[3:]
    width = gathered.shape[1]
    spaced = -(-capacity // 16) * 16
    which, tile = pl.program_id(0), pl.program_id(1)

    @pl.when((which == 0) & (tile == 0))
    def _():
        for i in range(count):
            gathered[i * tokens : (i + 1) * tokens, :] = rows[i][:, :width]
        total[...] = jnp.zeros_like(total)
        if backward and spaced != capacity:
            for kept in refs[1:3]:
                kept[...] = jnp.zeros_like(kept)

    @pl.when(tile == 0)
    def _():
        expert = scalars[which]
        columns = jnp.concatenate([r[:, width:] for r in rows], axis=0).astype(f32)
        lane = lax.broadcasted_iota(jnp.int32, columns.shape, 1)
        chosen = (lane == expert) | (lane == expert + experts)
        gate = jnp.sum(jnp.where(chosen, columns, 0.0), axis=1, keepdims=True)
        gate_of[...] = jnp.broadcast_to(gate, gate_of.shape)
        if backward:
            place = refs[0]
            total_rows = count * tokens
            slots = count * spaced
            row = lax.broadcasted_iota(jnp.int32, (total_rows, total_rows), 0)
            column = lax.broadcasted_iota(jnp.int32, (total_rows, total_rows), 1)
            earlier = column < row
            same = jnp.zeros_like(earlier)
            base = jnp.zeros((total_rows, slots), jnp.int32)
            placed_row = lax.broadcasted_iota(jnp.int32, (total_rows, slots), 0)
            for i in range(count):
                low, high = i * tokens, (i + 1) * tokens
                same = same | ((row >= low) & (row < high) & (column >= low) & (column < high))
                base = jnp.where(placed_row >= low, i * spaced, base)
            below = jnp.where(earlier & same, 1.0, 0.0).astype(bf16)
            routed = jnp.broadcast_to(jnp.where(gate > 0.0, 1.0, 0.0), (total_rows, slots))
            before = jnp.dot(below, routed.astype(bf16), preferred_element_type=f32)
            target = before.astype(jnp.int32) + base
            lane = lax.broadcasted_iota(jnp.int32, (total_rows, slots), 1)
            place[...] = jnp.where((lane == target) & (routed > 0.0), 1.0, 0.0).astype(bf16)

    def work(weights, kept):
        w_gate, w_up, w_down = weights
        gate = gate_of[:, 0:1]
        if not backward:
            value = gathered[...]
            gate_pre = jnp.dot(value, w_gate[...], preferred_element_type=f32)
            up_pre = jnp.dot(value, w_up[...], preferred_element_type=f32)
            act = (gate_pre * jax.nn.sigmoid(gate_pre) * (up_pre * gate)).astype(bf16)
            total[...] += jnp.dot(act, w_down[...], preferred_element_type=f32)
            return
        place, all_gate, all_up = refs[0], refs[1], refs[2]
        for i in range(count):
            all_gate[i * spaced : i * spaced + capacity, :] = kept[i][...]
            all_up[i * spaced : i * spaced + capacity, :] = kept[count + i][...]
        d_act = lax.dot_general(gathered[...], w_down[...], TURNED, preferred_element_type=f32)
        d_act = d_act * gate
        g = jnp.dot(place[...], all_gate[...], preferred_element_type=f32)
        u = jnp.dot(place[...], all_up[...], preferred_element_type=f32)
        q = jax.nn.sigmoid(g)
        d_gate = (d_act * u * q * (1.0 + g * (1.0 - q))).astype(bf16)
        d_up = (d_act * g * q).astype(bf16)
        total[...] += lax.dot_general(
            d_gate, w_gate[...], TURNED, preferred_element_type=f32
        ) + lax.dot_general(d_up, w_up[...], TURNED, preferred_element_type=f32)

    @pl.when(which == 0)
    def _():
        work(mine, kept_mine)

    @pl.when(which == 1)
    def _():
        work(theirs, kept_theirs)

    @pl.when((which == 1) & (tile == steps - 1))
    def _():
        for i in range(count):
            outs[i][...] = total[i * tokens : (i + 1) * tokens, :].astype(outs[i].dtype)


def run_experts(backward, experts, scalars, rows, mine, theirs, kept_mine, kept_theirs):
    count = len(rows)
    tokens = rows[0].shape[0]
    width, hidden = mine[0].shape[2:]
    steps = hidden // TILE
    capacity = kept_mine[0].shape[3]
    spaced = -(-capacity // 16) * 16

    def tile_of(turn):
        if turn == 0:
            return lambda which, tile: jnp.where(which == 0, tile, steps - 1)
        return lambda which, tile: jnp.where(which == 1, tile, 0)

    in_specs = [pl.BlockSpec(rows[0].shape, lambda which, tile, s: (0, 0)) for _ in rows]
    operands = list(rows)
    for turn, weights in enumerate((mine, theirs)):
        pick = tile_of(turn)
        for w in weights[:2]:
            in_specs.append(
                pl.BlockSpec(
                    (None, None, width, TILE),
                    lambda which, tile, s, pick=pick: (0, 0, 0, pick(which, tile)),
                )
            )
        in_specs.append(
            pl.BlockSpec(
                (None, None, TILE, width),
                lambda which, tile, s, pick=pick: (0, 0, pick(which, tile), 0),
            )
        )
        operands += list(weights)
    scratch = [
        pltpu.VMEM((count * tokens, width), bf16),
        pltpu.VMEM((count * tokens, width), f32),
        pltpu.VMEM((count * tokens, LANES), f32),
    ]
    if backward:
        for turn, kept in enumerate((kept_mine, kept_theirs)):
            pick = tile_of(turn)
            for array in kept:
                for i in range(count):
                    in_specs.append(
                        pl.BlockSpec(
                            (None, None, None, capacity, TILE),
                            lambda which, tile, s, pick=pick, i=i: (
                                0, 0, s[2 + i], 0, pick(which, tile),
                            ),
                        )
                    )
                    operands.append(array)
        scratch += [
            pltpu.VMEM((count * tokens, count * spaced), bf16),
            pltpu.VMEM((count * spaced, TILE), bf16),
            pltpu.VMEM((count * spaced, TILE), bf16),
        ]
    kinds = [f32 if i % 2 == 0 else bf16 for i in range(count)]
    amount = count * tokens * width * hidden
    return pl.pallas_call(
        functools.partial(
            experts_kernel, backward, experts, tokens, capacity, count, steps
        ),
        out_shape=[jax.ShapeDtypeStruct((tokens, width), kind) for kind in kinds],
        grid_spec=pltpu.PrefetchScalarGridSpec(
            num_scalar_prefetch=1,
            grid=(2, steps),
            in_specs=in_specs,
            out_specs=[pl.BlockSpec((tokens, width), lambda which, tile, s: (0, 0)) for _ in rows],
            scratch_shapes=scratch,
        ),
        compiler_params=pltpu.CompilerParams(
            dimension_semantics=("arbitrary", "arbitrary"), vmem_limit_bytes=40 * 1024 * 1024
        ),
        cost_estimate=pl.CostEstimate(
            flops=12 * amount, bytes_accessed=6 * width * hidden * 2, transcendentals=0
        ),
        name="experts_backward" if backward else "experts_forward",
    )(scalars, *operands)


def shards(
    x_forward,
    norm_gain,
    w_gate,
    w_up,
    w_down,
    ids_forward,
    gates_forward,
    x_backward,
    dy_backward,
    ids_backward,
    gates_backward,
    saved_gate,
    saved_up,
):
    experts = lax.axis_size("expert")
    sections = lax.axis_size("section")
    line = experts // 4
    me = lax.axis_index("expert")
    a, b, c = me // 4, (me // 2) % 2, me % 2

    def swap(value, bit):
        return lax.ppermute(value, "expert", [(i, i ^ bit) for i in range(experts)])

    def shift(value, steps):
        return lax.ppermute(
            value, "expert", [(i, (i + 4 * steps) % experts) for i in range(experts)]
        )

    def relay(value, section_steps, steps=0):
        pairs = []
        for s in range(sections):
            for i in range(experts):
                target = ((s + section_steps) % sections) * experts + (i + 4 * steps) % experts
                pairs.append((s * experts + i, target))
        return lax.ppermute(value, ("section", "expert"), pairs)

    order = []
    for k in range(1, line // 2 + 1):
        order += [k] if 2 * k == line else [k, line - k]
    order.append(0)
    chunks = [order[i : i + 2] for i in range(0, line, 2)]

    def gather(payload):
        held = {0: payload}
        for k in order[:-1]:
            held[k] = shift(held[k - 1], 1) if 2 * k <= line else shift(held[(k + 1) % line], -1)
        return {k: (held[k], swap(held[k], 2)) for k in order}

    def block_of(k, other):
        return (((a - k) % line) * 2 + (b ^ other)) * 2 + c

    mine = (w_gate, w_up, w_down)
    theirs = tuple(swap(w, 1) for w in mine)
    kept_mine = (saved_gate, saved_up)
    kept_theirs = tuple(swap(s, 1) for s in kept_mine)

    def experts_on(backward, arrived):
        pieces = {}
        for chunk in chunks:
            scalars = jnp.stack([me, me ^ 1] + [block_of(k, o) for k in chunk for o in (0, 1)])
            rows = [arrived[k][o] for k in chunk for o in (0, 1)]
            out = run_experts(
                backward, experts, scalars.astype(jnp.int32), rows, mine, theirs, kept_mine, kept_theirs
            )
            for i, k in enumerate(chunk):
                pieces[k] = (out[2 * i], out[2 * i + 1])
        return pieces

    def scatter(pieces, section_steps):
        total = None
        for k in order:
            chip = pieces[k][0] + swap(pieces[k][1], 2).astype(f32)
            came = relay(chip.astype(bf16), section_steps, -k).astype(f32)
            total = came if total is None else total + came
        return total

    input_rows = x_forward[0]
    normed = input_rows.astype(f32) * inverse_rms(input_rows) * norm_gain[0][None, :]
    payload_b = jnp.concatenate(
        [dy_backward[0], gate_columns(ids_backward[0], gates_backward[0], experts)], axis=1
    )
    payload_f = jnp.concatenate(
        [normed.astype(bf16), gate_columns(ids_forward[0], gates_forward[0], experts)], axis=1
    )
    residual = relay(input_rows, 1)
    saved_input = relay(x_backward[0], -1).astype(f32)
    gradient = relay(dy_backward[0], -1)
    gain = relay(norm_gain, -1)[0]

    arrived_b = gather(payload_b)
    arrived_f = gather(payload_f)

    d_normed = scatter(experts_on(True, arrived_b), -1)
    scale_rows = inverse_rms(saved_input)
    weighted = d_normed * gain[None, :]
    inner = jnp.mean(weighted * saved_input, axis=-1, keepdims=True)
    next_backward = (
        gradient.astype(f32)
        + scale_rows * weighted
        - saved_input * scale_rows * scale_rows * scale_rows * inner
    ).astype(bf16)

    combined = scatter(experts_on(False, arrived_f), 1)
    next_forward = (residual.astype(f32) + combined).astype(bf16)
    return (next_forward[None], next_backward[None])


def solution(mesh):
    rows = P("section", "expert", None)
    weights = P("section", "expert", None, None)
    saved = P("section", "expert", None, None, None)
    placed = (
        rows, P("section", None), weights, weights, weights, rows, rows,
        rows, rows, rows, rows, saved, saved,
    )
    return jax.shard_map(
        shards, mesh=mesh, in_specs=placed, out_specs=(rows, rows), check_vma=False
    )
```

```python
import functools

import jax
import jax.numpy as jnp
from jax import lax
from jax.experimental import pallas as pl
from jax.experimental.pallas import tpu as pltpu
from jax.sharding import PartitionSpec as P

epsilon = 1e-06
f32 = jnp.float32
bf16 = jnp.bfloat16
LANES = 128
TILE = 256
OWN = f32
VMEM_LIMIT = 56 * 1024 * 1024
PACK_VMEM_LIMIT = 56 * 1024 * 1024
TURNED = (((1,), (1,)), ((), ()))


def inverse_rms(values):
    widened = values.astype(f32)
    return lax.rsqrt(jnp.mean(widened * widened, axis=-1, keepdims=True) + epsilon)


def pack_kernel(experts, dy, x, gain, ids_b, gates_b, ids_f, gates_f, x_b, out_b, out_f, pair):
    tokens, width = dy.shape
    wide = x[...].astype(f32)
    scale = lax.rsqrt(jnp.mean(wide * wide, axis=-1, keepdims=True) + epsilon)
    pair[:tokens, :] = x_b[...]
    pair[tokens:, :] = dy[...]
    values = (dy[...], (wide * scale * gain[...]).astype(bf16))
    spread = (experts, out_b.shape[1] - width)
    row = lax.broadcasted_iota(jnp.int32, spread, 0)
    lane = lax.broadcasted_iota(jnp.int32, spread, 1)
    first = jnp.where(lane == row, 1.0, 0.0).astype(bf16)
    second = jnp.where(lane == row + experts, 1.0, 0.0).astype(bf16)
    expert = lax.broadcasted_iota(jnp.int32, (experts, tokens), 0)
    turned = (((0,), (0,)), ((), ()))
    for i, (ids, gates, out) in enumerate(((ids_b, gates_b, out_b), (ids_f, gates_f, out_f))):
        dense = jnp.zeros((experts, tokens), f32)
        for k in range(ids.shape[0]):
            dense = dense + jnp.where(expert == ids[k : k + 1, :], gates[k : k + 1, :], 0.0)
        high = dense.astype(bf16)
        low = (dense - high.astype(f32)).astype(bf16)
        columns = lax.dot_general(high, first, turned, preferred_element_type=f32)
        columns += lax.dot_general(low, second, turned, preferred_element_type=f32)
        out[:, :width] = values[i]
        out[:, width:] = columns.astype(bf16)


def pack(experts, dy, x, gain, ids_b, gates_b, ids_f, gates_f, x_b):
    tokens, width = dy.shape
    columns = -(-2 * experts // LANES) * LANES
    vmem = pl.BlockSpec(memory_space=pltpu.VMEM)
    one = jax.ShapeDtypeStruct((tokens, width + columns), bf16)
    return pl.pallas_call(
        functools.partial(pack_kernel, experts),
        out_shape=[one, one, jax.ShapeDtypeStruct((2 * tokens, width), bf16)],
        in_specs=[vmem] * 8,
        out_specs=[vmem] * 3,
        compiler_params=pltpu.CompilerParams(vmem_limit_bytes=PACK_VMEM_LIMIT),
        name="pack",
    )(dy, x, gain, ids_b.T, gates_b.T, ids_f.T, gates_f.T, x_b)


def experts_kernel(backward, experts, tokens, capacity, chunk, apart, starts, table, *refs):
    count = len(starts)
    rows, refs = refs[:count], refs[count:]
    weights, refs = (refs[:3], refs[3:6]), refs[6:]
    if backward:
        kept, gain, refs = (refs[:2], refs[2:4]), refs[4], refs[5:]
    outs, refs = refs[: count // 2], refs[count // 2 :]
    sent, refs = (refs[: count // 2], refs[count // 2 :]) if apart else (refs[:1], refs[1:])
    gathered, columns_of, hidden, gates_ups, downs, sems = refs[:6]
    amount = count * tokens
    width = gathered.shape[1]
    inner = hidden.shape[1] // (4 if backward else 2)
    spaced = -(-capacity // 16) * 16
    slots = count * spaced

    copies = []

    def fetch(source, target):
        copies.append(pltpu.make_async_copy(source, target, sems.at[len(copies)]))
        copies[-1].start()
        return copies[-1]

    def fetch_first(e):
        if not backward:
            return [fetch(weights[e][j].at[0, 0], gates_ups.at[e, j]) for j in range(2)]
        group = [fetch(weights[e][2].at[0, 0], downs.at[e])]
        for i in range(count):
            block = table[chunk, 2 + i]
            for j in range(2):
                to = refs[6].at[e, j, i * spaced : i * spaced + capacity, :]
                group.append(fetch(kept[e][j].at[0, 0, block], to))
        return group

    def fetch_second(e):
        if not backward:
            return [fetch(weights[e][2].at[0, 0], downs.at[e])]
        return [fetch(weights[e][j].at[0, 0], gates_ups.at[e, j]) for j in range(2)]

    if backward and spaced != capacity:
        refs[6][...] = jnp.zeros_like(refs[6])
    group = []
    for i in range(count):
        here = slice(i * tokens, (i + 1) * tokens)
        source = slice(starts[i], starts[i] + tokens)
        group.append(fetch(rows[i].at[source, :width], gathered.at[here, :]))
        group.append(fetch(rows[i].at[source, width:], columns_of.at[here, :]))
    groups = [group, fetch_first(0), fetch_first(1)]
    for copy in groups[0]:
        copy.wait()

    columns = columns_of[...].astype(f32)
    lane = lax.broadcasted_iota(jnp.int32, columns.shape, 1)
    if backward:
        row = lax.broadcasted_iota(jnp.int32, (amount, amount), 0)
        column = lax.broadcasted_iota(jnp.int32, (amount, amount), 1)
        below = column < row
        placed_row = lax.broadcasted_iota(jnp.int32, (amount, slots), 0)
        base = jnp.zeros((amount, slots), jnp.int32)
        for i in range(1, count):
            below = below & ((row < i * tokens) | (column >= i * tokens))
            base = jnp.where(placed_row >= i * tokens, i * spaced, base)
        below = jnp.where(below, 1.0, 0.0).astype(bf16)
        slot_lane = lax.broadcasted_iota(jnp.int32, (amount, slots), 1)

    for e in range(2):
        expert = table[chunk, e]
        chosen = (lane == expert) | (lane == expert + experts)
        gate = jnp.sum(jnp.where(chosen, columns, 0.0), axis=1, keepdims=True)
        if backward:
            routed = jnp.broadcast_to(jnp.where(gate > 0.0, 1.0, 0.0), (amount, slots))
            before = jnp.dot(below, routed.astype(bf16), preferred_element_type=f32)
            target = before.astype(jnp.int32) + base
            place = jnp.where((slot_lane == target) & (routed > 0.0), 1.0, 0.0).astype(bf16)
        for copy in groups[1 + e]:
            copy.wait()
        groups.append(fetch_second(e))
        value = gathered[...]
        if not backward:
            gate_pre = jnp.dot(value, gates_ups[e, 0], preferred_element_type=f32)
            up_pre = jnp.dot(value, gates_ups[e, 1], preferred_element_type=f32)
            act = gate_pre * jax.nn.sigmoid(gate_pre) * (up_pre * gate)
            hidden[:, e * inner : (e + 1) * inner] = act.astype(bf16)
            continue
        d_act = gate * lax.dot_general(value, downs[e], TURNED, preferred_element_type=f32)
        g = jnp.dot(place, refs[6][e, 0], preferred_element_type=f32)
        u = jnp.dot(place, refs[6][e, 1], preferred_element_type=f32)
        q = jax.nn.sigmoid(g)
        at = 2 * e * inner
        hidden[:, at : at + inner] = (d_act * u * q * (1.0 + g * (1.0 - q))).astype(bf16)
        hidden[:, at + inner : at + 2 * inner] = (d_act * g * q).astype(bf16)

    total = None
    for e in range(2):
        for copy in groups[3 + e]:
            copy.wait()
        if backward:
            for j in range(2):
                left = hidden[:, (2 * e + j) * inner : (2 * e + j + 1) * inner]
                term = lax.dot_general(left, gates_ups[e, j], TURNED, preferred_element_type=f32)
                total = term if total is None else total + term
        else:
            left = hidden[:, e * inner : (e + 1) * inner]
            term = jnp.dot(left, downs[e], preferred_element_type=f32)
            total = term if total is None else total + term
    if backward:
        total = total * gain[...]
    for i in range(count):
        piece = total[i * tokens : (i + 1) * tokens, :]
        if i % 2 == 0:
            outs[i // 2][...] = piece.astype(outs[i // 2].dtype)
        else:
            at = 0 if apart else i // 2 * tokens
            sent[i // 2 if apart else 0][at : at + tokens, :] = piece.astype(bf16)


def run_experts(backward, experts, tokens, chunk, apart, table, rows, mine, theirs, kept_mine, kept_theirs, gain):
    count = len(rows)
    starts = [start for _, start in rows]
    rows = [array for array, _ in rows]
    width, inner = mine[0].shape[2:]
    capacity = kept_mine[0].shape[3]
    spaced = -(-capacity // 16) * 16
    vmem, anywhere = pl.BlockSpec(memory_space=pltpu.VMEM), pl.BlockSpec(memory_space=pl.ANY)
    operands = list(rows) + list(mine) + list(theirs)
    copies = 2 * count + 6
    scratch = [
        pltpu.VMEM((count * tokens, width), bf16),
        pltpu.VMEM((count * tokens, rows[0].shape[1] - width), bf16),
        pltpu.VMEM((count * tokens, (4 if backward else 2) * inner), bf16),
        pltpu.VMEM((2, 2, width, inner), bf16),
        pltpu.VMEM((2, inner, width), bf16),
    ]
    in_specs = [pl.BlockSpec(memory_space=pltpu.SMEM)] + [anywhere] * len(operands)
    if backward:
        operands += list(kept_mine) + list(kept_theirs) + [gain]
        in_specs += [anywhere] * 4 + [vmem]
        copies += 4 * count
    scratch.append(pltpu.SemaphoreType.DMA((copies,)))
    if backward:
        scratch.append(pltpu.VMEM((2, 2, count * spaced, inner), bf16))
    out_shape = [jax.ShapeDtypeStruct((tokens, width), OWN)] * (count // 2)
    if apart:
        out_shape += [jax.ShapeDtypeStruct((tokens, width), bf16)] * (count // 2)
    else:
        out_shape += [jax.ShapeDtypeStruct((count // 2 * tokens, width), bf16)]
    return pl.pallas_call(
        functools.partial(
            experts_kernel, backward, experts, tokens, capacity, chunk, apart, starts
        ),
        out_shape=out_shape,
        in_specs=in_specs,
        out_specs=[vmem] * len(out_shape),
        scratch_shapes=scratch,
        compiler_params=pltpu.CompilerParams(vmem_limit_bytes=VMEM_LIMIT),
        cost_estimate=pl.CostEstimate(
            flops=12 * count * tokens * width * inner,
            bytes_accessed=12 * width * inner,
            transcendentals=0,
        ),
        name="experts_backward" if backward else "experts_forward",
    )(table, *operands)


def shards(
    x_forward,
    norm_gain,
    w_gate,
    w_up,
    w_down,
    ids_forward,
    gates_forward,
    x_backward,
    dy_backward,
    ids_backward,
    gates_backward,
    saved_gate,
    saved_up,
):
    experts = lax.axis_size("expert")
    sections = lax.axis_size("section")
    line = experts // 4
    me = lax.axis_index("expert")
    a, b, c = me // 4, (me // 2) % 2, me % 2

    def swap(value, bit, label):
        with jax.named_scope(label):
            return lax.ppermute(value, "expert", [(i, i ^ bit) for i in range(experts)])

    def shift(value, steps, label):
        with jax.named_scope(label):
            return lax.ppermute(
                value, "expert", [(i, (i + 4 * steps) % experts) for i in range(experts)]
            )

    def relay(value, section_steps, label, steps=0):
        pairs = []
        for s in range(sections):
            for i in range(experts):
                target = ((s + section_steps) % sections) * experts + (i + 4 * steps) % experts
                pairs.append((s * experts + i, target))
        with jax.named_scope(label):
            return lax.ppermute(value, ("section", "expert"), pairs)

    order = [0, 1]
    for k in range(2, line // 2 + 1):
        order += [k, line + 1 - k]
    chunks = [order[i : i + 2] for i in range(0, line, 2)]
    last = len(chunks) - 1

    def after(value, *others):
        return lax.optimization_barrier((value,) + others)[0]

    def farther(held, k, label):
        if 2 * k <= line:
            return shift(held[k - 1], 1, f"T_{label}_z{k}")
        return shift(held[(k + 1) % line], -1, f"T_{label}_z{k}")

    def block_of(k, other):
        return (((a - k) % line) * 2 + (b ^ other)) * 2 + c

    def scalars_of(chunk):
        blocks = [block_of(k, o) for k in chunk for o in (0, 1)]
        return jnp.stack([me, me ^ 1] + blocks).astype(jnp.int32)

    gain = norm_gain
    input_rows = x_forward[0]
    tokens = input_rows.shape[0]
    table = jnp.stack([scalars_of(chunk) for chunk in chunks])
    packed = pack(
        experts, dy_backward[0], input_rows, gain,
        ids_backward[0], gates_backward[0], ids_forward[0], gates_forward[0], x_backward[0],
    )
    held = {True: {0: packed[0]}, False: {0: packed[1]}}
    across = {True: {}, False: {}}
    names = {True: "b", False: "f"}

    def go_along(backward, i, *earlier):
        before, moved = held[backward], []
        ready = {k: after(v, *earlier) for k, v in before.items()}
        for k in chunks[i]:
            if k:
                before[k] = farther(ready, k, names[backward])
                moved.append(before[k])
        return moved

    def go_across(backward, ks, *earlier):
        moved = []
        for k in ks:
            value = swap(after(held[backward][k], *earlier), 2, f"T_{names[backward]}_x{k}")
            across[backward][k] = value
            moved.append(value)
        return moved

    def experts_on(backward, i, *earlier):
        chunk, apart = chunks[i], not backward and i == last
        rows = [(r, 0) for k in chunk for r in (held[backward][k], across[backward][k])]
        out = run_experts(
            backward, experts, tokens, i, apart, after(table, *earlier), rows,
            mine, theirs, kept_mine, kept_theirs, gain,
        )
        return dict(zip(chunk, out)), out[len(chunk) :]

    def chip_sums(chunk, own, sent, label, *earlier):
        came = swap(after(sent[0], *earlier), 2, label)
        return {
            k: (own[k] + came[i * tokens : (i + 1) * tokens].astype(f32)).astype(bf16)
            for i, k in enumerate(chunk)
        }, came

    def send_sums(backward, sums, *earlier):
        moved = []
        for k, value in sums.items():
            label = f"T_{names[backward]}_r{k}"
            moved.append(relay(after(value, *earlier), -1 if backward else 1, label, -k))
        return moved

    wave = go_along(True, 0) + go_across(True, [0]) + go_across(False, [0])
    theirs_gate = swap(after(w_gate, packed[0]), 1, "T_wg")
    theirs_up = swap(after(w_up, packed[0]), 1, "T_wu")
    wave += [theirs_gate, theirs_up]
    table = after(table, *wave)
    theirs_down = swap(after(w_down, *wave), 1, "T_wd")
    theirs_kept_gate = swap(after(saved_gate, *wave), 1, "T_sg")
    theirs_kept_up = swap(after(saved_up, *wave), 1, "T_su")
    near = go_across(True, chunks[0][1:], *wave)
    wave = near + [theirs_down, theirs_kept_gate, theirs_kept_up]
    flying = go_along(True, 1)
    mine, theirs = (w_gate, w_up, w_down), (theirs_gate, theirs_up, theirs_down)
    kept_mine, kept_theirs = (saved_gate, saved_up), (theirs_kept_gate, theirs_kept_up)

    steps = [(True, i) for i in range(last + 1)] + [(False, i) for i in range(last + 1)]
    half = last + 1
    runs, sums, ends = {}, {}, {}
    came = {True: [], False: []}
    for p, (backward, i) in enumerate(steps):
        if backward and i:
            wave += go_across(True, chunks[i], *wave)
        moved, flying = flying, []
        if p == 0:
            moved += go_along(False, 0, *wave)
            pair = relay(after(packed[2], *wave), -1, "T_y2")
            moved.append(pair)
        if backward and 0 < i < last:
            moved += go_along(True, i + 1, *wave)
        ahead, side = p - half + 2, p - half + 1
        if 1 <= ahead <= last:
            moved += go_along(False, ahead, *wave)
        if 0 <= side <= last:
            moved += go_across(False, [k for k in chunks[side] if k], *wave)
        if p == half - 1:
            ends["residual"] = relay(after(input_rows, *wave), 1, "T_y1")
            moved.append(ends["residual"])
        if p >= 2:
            way, j = steps[p - 2]
            moved += send_sums(way, sums[p - 2], *wave)
            came[way] += moved[-len(chunks[j]) :]
        if p:
            way, j = steps[p - 1]
            sums[p - 1], arrived = chip_sums(
                chunks[j], *runs[p - 1], f"T_{names[way]}_s{j}", *wave
            )
            moved.append(arrived)
        runs[p] = experts_on(backward, i, *wave)
        wave = moved + list(runs[p][1])
    p = len(steps)
    came[False] += send_sums(False, sums[p - 2], *wave)
    own, sent = runs[p - 1]
    for k, value in zip(chunks[last], sent):
        arrived = swap(after(value, *wave), 2, f"T_f_s{k}")
        chip = (own[k] + arrived.astype(f32)).astype(bf16)
        came[False] += send_sums(False, {k: chip})
        wave = [arrived]

    def summed(values):
        total = values[0].astype(f32)
        for value in values[1:]:
            total = total + value.astype(f32)
        return total

    residual = ends["residual"].astype(f32)
    saved_input, gradient = pair[:tokens].astype(f32), pair[tokens:].astype(f32)
    weighted = summed(came[True])
    scale_rows = inverse_rms(saved_input)
    inner = jnp.mean(weighted * saved_input, axis=-1, keepdims=True)
    next_backward = (
        gradient
        + scale_rows * weighted
        - saved_input * scale_rows * scale_rows * scale_rows * inner
    ).astype(bf16)

    combined = summed(came[False])
    next_forward = (residual + combined).astype(bf16)
    return (next_forward[None], next_backward[None])


def solution(mesh):
    rows = P("section", "expert", None)
    weights = P("section", "expert", None, None)
    saved = P("section", "expert", None, None, None)
    placed = (
        rows, P("section", None), weights, weights, weights, rows, rows,
        rows, rows, rows, rows, saved, saved,
    )
    return jax.shard_map(
        shards, mesh=mesh, in_specs=placed, out_specs=(rows, rows), check_vma=False
    )
```

```python
import functools

import jax
import jax.numpy as jnp
from jax import lax
from jax.experimental import pallas as pl
from jax.experimental.pallas import tpu as pltpu
from jax.sharding import PartitionSpec as P

epsilon = 1e-06
f32 = jnp.float32
bf16 = jnp.bfloat16
LANES = 128
TILE = 256
OWN = f32
VMEM_LIMIT = 56 * 1024 * 1024
PACK_VMEM_LIMIT = 56 * 1024 * 1024
TURNED = (((1,), (1,)), ((), ()))


def inverse_rms(values):
    widened = values.astype(f32)
    return lax.rsqrt(jnp.mean(widened * widened, axis=-1, keepdims=True) + epsilon)


def pack_kernel(experts, dy, x, gain, ids_b, gates_b, ids_f, gates_f, out_b, out_f):
    tokens, width = dy.shape
    wide = x[...].astype(f32)
    scale = lax.rsqrt(jnp.mean(wide * wide, axis=-1, keepdims=True) + epsilon)
    values = (dy[...], (wide * scale * gain[...]).astype(bf16))
    spread = (experts, out_b.shape[1] - width)
    row = lax.broadcasted_iota(jnp.int32, spread, 0)
    lane = lax.broadcasted_iota(jnp.int32, spread, 1)
    first = jnp.where(lane == row, 1.0, 0.0).astype(bf16)
    second = jnp.where(lane == row + experts, 1.0, 0.0).astype(bf16)
    expert = lax.broadcasted_iota(jnp.int32, (experts, tokens), 0)
    turned = (((0,), (0,)), ((), ()))
    for i, (ids, gates, out) in enumerate(((ids_b, gates_b, out_b), (ids_f, gates_f, out_f))):
        dense = jnp.zeros((experts, tokens), f32)
        for k in range(ids.shape[0]):
            dense = dense + jnp.where(expert == ids[k : k + 1, :], gates[k : k + 1, :], 0.0)
        high = dense.astype(bf16)
        low = (dense - high.astype(f32)).astype(bf16)
        columns = lax.dot_general(high, first, turned, preferred_element_type=f32)
        columns += lax.dot_general(low, second, turned, preferred_element_type=f32)
        out[:, :width] = values[i]
        out[:, width:] = columns.astype(bf16)


def pack(experts, dy, x, gain, ids_b, gates_b, ids_f, gates_f):
    tokens, width = dy.shape
    columns = -(-2 * experts // LANES) * LANES
    vmem = pl.BlockSpec(memory_space=pltpu.VMEM)
    one = jax.ShapeDtypeStruct((tokens, width + columns), bf16)
    return pl.pallas_call(
        functools.partial(pack_kernel, experts),
        out_shape=[one, one],
        in_specs=[vmem] * 7,
        out_specs=[vmem] * 2,
        compiler_params=pltpu.CompilerParams(vmem_limit_bytes=PACK_VMEM_LIMIT),
        name="pack",
    )(dy, x, gain, ids_b.T, gates_b.T, ids_f.T, gates_f.T)


def experts_kernel(backward, experts, tokens, capacity, chunk, apart, starts, table, *refs):
    count = len(starts)
    rows, refs = refs[:count], refs[count:]
    weights, refs = (refs[:3], refs[3:6]), refs[6:]
    if backward:
        kept, gain, refs = (refs[:2], refs[2:4]), refs[4], refs[5:]
    outs, refs = refs[: count // 2], refs[count // 2 :]
    sent, refs = (refs[: count // 2], refs[count // 2 :]) if apart else (refs[:1], refs[1:])
    gathered, columns_of, hidden, gates_ups, downs, sems = refs[:6]
    amount = count * tokens
    width = gathered.shape[1]
    inner = hidden.shape[1] // (4 if backward else 2)
    spaced = -(-capacity // 16) * 16
    slots = count * spaced

    copies = []

    def fetch(source, target):
        copies.append(pltpu.make_async_copy(source, target, sems.at[len(copies)]))
        copies[-1].start()
        return copies[-1]

    def fetch_first(e):
        if not backward:
            return [fetch(weights[e][j].at[0, 0], gates_ups.at[e, j]) for j in range(2)]
        group = [fetch(weights[e][2].at[0, 0], downs.at[e])]
        for i in range(count):
            block = table[chunk, 2 + i]
            for j in range(2):
                to = refs[6].at[e, j, i * spaced : i * spaced + capacity, :]
                group.append(fetch(kept[e][j].at[0, 0, block], to))
        return group

    def fetch_second(e):
        if not backward:
            return [fetch(weights[e][2].at[0, 0], downs.at[e])]
        return [fetch(weights[e][j].at[0, 0], gates_ups.at[e, j]) for j in range(2)]

    if backward and spaced != capacity:
        refs[6][...] = jnp.zeros_like(refs[6])
    group = []
    for i in range(count):
        here = slice(i * tokens, (i + 1) * tokens)
        source = slice(starts[i], starts[i] + tokens)
        group.append(fetch(rows[i].at[source, :width], gathered.at[here, :]))
        group.append(fetch(rows[i].at[source, width:], columns_of.at[here, :]))
    groups = [group, fetch_first(0), fetch_first(1)]
    for copy in groups[0]:
        copy.wait()

    columns = columns_of[...].astype(f32)
    lane = lax.broadcasted_iota(jnp.int32, columns.shape, 1)
    if backward:
        row = lax.broadcasted_iota(jnp.int32, (amount, amount), 0)
        column = lax.broadcasted_iota(jnp.int32, (amount, amount), 1)
        below = column < row
        placed_row = lax.broadcasted_iota(jnp.int32, (amount, slots), 0)
        base = jnp.zeros((amount, slots), jnp.int32)
        for i in range(1, count):
            below = below & ((row < i * tokens) | (column >= i * tokens))
            base = jnp.where(placed_row >= i * tokens, i * spaced, base)
        below = jnp.where(below, 1.0, 0.0).astype(bf16)
        slot_lane = lax.broadcasted_iota(jnp.int32, (amount, slots), 1)

    for e in range(2):
        expert = table[chunk, e]
        chosen = (lane == expert) | (lane == expert + experts)
        gate = jnp.sum(jnp.where(chosen, columns, 0.0), axis=1, keepdims=True)
        if backward:
            routed = jnp.broadcast_to(jnp.where(gate > 0.0, 1.0, 0.0), (amount, slots))
            before = jnp.dot(below, routed.astype(bf16), preferred_element_type=f32)
            target = before.astype(jnp.int32) + base
            place = jnp.where((slot_lane == target) & (routed > 0.0), 1.0, 0.0).astype(bf16)
        for copy in groups[1 + e]:
            copy.wait()
        groups.append(fetch_second(e))
        value = gathered[...]
        if not backward:
            gate_pre = jnp.dot(value, gates_ups[e, 0], preferred_element_type=f32)
            up_pre = jnp.dot(value, gates_ups[e, 1], preferred_element_type=f32)
            act = gate_pre * jax.nn.sigmoid(gate_pre) * (up_pre * gate)
            hidden[:, e * inner : (e + 1) * inner] = act.astype(bf16)
            continue
        d_act = gate * lax.dot_general(value, downs[e], TURNED, preferred_element_type=f32)
        g = jnp.dot(place, refs[6][e, 0], preferred_element_type=f32)
        u = jnp.dot(place, refs[6][e, 1], preferred_element_type=f32)
        q = jax.nn.sigmoid(g)
        at = 2 * e * inner
        hidden[:, at : at + inner] = (d_act * u * q * (1.0 + g * (1.0 - q))).astype(bf16)
        hidden[:, at + inner : at + 2 * inner] = (d_act * g * q).astype(bf16)

    total = None
    for e in range(2):
        for copy in groups[3 + e]:
            copy.wait()
        if backward:
            for j in range(2):
                left = hidden[:, (2 * e + j) * inner : (2 * e + j + 1) * inner]
                term = lax.dot_general(left, gates_ups[e, j], TURNED, preferred_element_type=f32)
                total = term if total is None else total + term
        else:
            left = hidden[:, e * inner : (e + 1) * inner]
            term = jnp.dot(left, downs[e], preferred_element_type=f32)
            total = term if total is None else total + term
    if backward:
        total = total * gain[...]
    for i in range(count):
        piece = total[i * tokens : (i + 1) * tokens, :]
        if i % 2 == 0:
            outs[i // 2][...] = piece.astype(outs[i // 2].dtype)
        else:
            at = 0 if apart else i // 2 * tokens
            sent[i // 2 if apart else 0][at : at + tokens, :] = piece.astype(bf16)


def run_experts(backward, experts, tokens, chunk, apart, table, rows, mine, theirs, kept_mine, kept_theirs, gain):
    count = len(rows)
    starts = [start for _, start in rows]
    rows = [array for array, _ in rows]
    width, inner = mine[0].shape[2:]
    capacity = kept_mine[0].shape[3]
    spaced = -(-capacity // 16) * 16
    vmem, anywhere = pl.BlockSpec(memory_space=pltpu.VMEM), pl.BlockSpec(memory_space=pl.ANY)
    operands = list(rows) + list(mine) + list(theirs)
    copies = 2 * count + 6
    scratch = [
        pltpu.VMEM((count * tokens, width), bf16),
        pltpu.VMEM((count * tokens, rows[0].shape[1] - width), bf16),
        pltpu.VMEM((count * tokens, (4 if backward else 2) * inner), bf16),
        pltpu.VMEM((2, 2, width, inner), bf16),
        pltpu.VMEM((2, inner, width), bf16),
    ]
    in_specs = [pl.BlockSpec(memory_space=pltpu.SMEM)] + [anywhere] * len(operands)
    if backward:
        operands += list(kept_mine) + list(kept_theirs) + [gain]
        in_specs += [anywhere] * 4 + [vmem]
        copies += 4 * count
    scratch.append(pltpu.SemaphoreType.DMA((copies,)))
    if backward:
        scratch.append(pltpu.VMEM((2, 2, count * spaced, inner), bf16))
    out_shape = [jax.ShapeDtypeStruct((tokens, width), OWN)] * (count // 2)
    if apart:
        out_shape += [jax.ShapeDtypeStruct((tokens, width), bf16)] * (count // 2)
    else:
        out_shape += [jax.ShapeDtypeStruct((count // 2 * tokens, width), bf16)]
    return pl.pallas_call(
        functools.partial(
            experts_kernel, backward, experts, tokens, capacity, chunk, apart, starts
        ),
        out_shape=out_shape,
        in_specs=in_specs,
        out_specs=[vmem] * len(out_shape),
        scratch_shapes=scratch,
        compiler_params=pltpu.CompilerParams(vmem_limit_bytes=VMEM_LIMIT),
        cost_estimate=pl.CostEstimate(
            flops=12 * count * tokens * width * inner,
            bytes_accessed=12 * width * inner,
            transcendentals=0,
        ),
        name="experts_backward" if backward else "experts_forward",
    )(table, *operands)


def shards(
    x_forward,
    norm_gain,
    w_gate,
    w_up,
    w_down,
    ids_forward,
    gates_forward,
    x_backward,
    dy_backward,
    ids_backward,
    gates_backward,
    saved_gate,
    saved_up,
):
    experts = lax.axis_size("expert")
    sections = lax.axis_size("section")
    line = experts // 4
    me = lax.axis_index("expert")
    a, b, c = me // 4, (me // 2) % 2, me % 2

    def swap(value, bit, label):
        with jax.named_scope(label):
            return lax.ppermute(value, "expert", [(i, i ^ bit) for i in range(experts)])

    def shift(value, steps, label):
        with jax.named_scope(label):
            return lax.ppermute(
                value, "expert", [(i, (i + 4 * steps) % experts) for i in range(experts)]
            )

    def relay(value, section_steps, label, steps=0):
        pairs = []
        for s in range(sections):
            for i in range(experts):
                target = ((s + section_steps) % sections) * experts + (i + 4 * steps) % experts
                pairs.append((s * experts + i, target))
        with jax.named_scope(label):
            return lax.ppermute(value, ("section", "expert"), pairs)

    order = [0, 1]
    for k in range(2, line // 2 + 1):
        order += [k, line + 1 - k]
    chunks = [order[i : i + 2] for i in range(0, line, 2)]
    last = len(chunks) - 1

    def after(value, *others):
        return lax.optimization_barrier((value,) + others)[0]

    def farther(held, k, label):
        if 2 * k <= line:
            return shift(held[k - 1], 1, f"T_{label}_z{k}")
        return shift(held[(k + 1) % line], -1, f"T_{label}_z{k}")

    def block_of(k, other):
        return (((a - k) % line) * 2 + (b ^ other)) * 2 + c

    def scalars_of(chunk):
        blocks = [block_of(k, o) for k in chunk for o in (0, 1)]
        return jnp.stack([me, me ^ 1] + blocks).astype(jnp.int32)

    gain = norm_gain
    input_rows = x_forward[0]
    tokens = input_rows.shape[0]
    table = jnp.stack([scalars_of(chunk) for chunk in chunks])
    packed = pack(
        experts, dy_backward[0], input_rows, gain,
        ids_backward[0], gates_backward[0], ids_forward[0], gates_forward[0],
    )
    held = {True: {0: packed[0]}, False: {0: packed[1]}}
    across = {True: {}, False: {}}
    names = {True: "b", False: "f"}

    def along(backward, k, *earlier):
        ready = {j: after(v, *earlier) for j, v in held[backward].items()}
        held[backward][k] = farther(ready, k, names[backward])
        return [held[backward][k]]

    def aside(backward, k, *earlier):
        known, name = across[backward], names[backward]
        if 2 * k <= line:
            known[k] = swap(after(held[backward][k], *earlier), 2, f"T_{name}_x{k}")
        else:
            known[k] = shift(after(known[(k + 1) % line], *earlier), -1, f"T_{name}_w{k}")
        return [known[k]]

    def experts_on(backward, i, *earlier):
        chunk, apart = chunks[i], not backward and i == last
        rows = [(r, 0) for k in chunk for r in (held[backward][k], across[backward][k])]
        out = run_experts(
            backward, experts, tokens, i, apart, after(table, *earlier), rows,
            mine, theirs, kept_mine, kept_theirs, gain,
        )
        return dict(zip(chunk, out)), out[len(chunk) :]

    def chip_sum(backward, k, own, piece):
        total = own + piece.astype(f32)
        return total if backward and k == 0 else total.astype(bf16)

    def chip_sums(backward, chunk, own, sent, label, *earlier):
        came = swap(after(sent[0], *earlier), 2, label)
        pieces = {k: came[i * tokens : (i + 1) * tokens] for i, k in enumerate(chunk)}
        return {k: chip_sum(backward, k, own[k], piece) for k, piece in pieces.items()}, came

    def send_sums(backward, sums, *earlier):
        moved = []
        for k, value in sums.items():
            label, value = f"T_{names[backward]}_r{k}", after(value, *earlier)
            if not backward:
                moved.append(relay(value, 1, label, -k))
            elif k:
                moved.append(shift(value, -k, label))
            else:
                came[True].append(value)
        came[backward].extend(moved)
        return moved

    near, far = chunks[0][1], chunks[-1][-1]
    wave = along(True, near) + aside(True, 0)
    theirs_gate = swap(after(w_gate, packed[0]), 1, "T_wg")
    theirs_up = swap(after(w_up, packed[0]), 1, "T_wu")
    theirs_kept_gate = swap(after(saved_gate, packed[0]), 1, "T_sg")
    wave += [theirs_gate, theirs_up, theirs_kept_gate]
    table = after(table, *wave)
    theirs_down = swap(after(w_down, *wave), 1, "T_wd")
    theirs_kept_up = swap(after(saved_up, *wave), 1, "T_su")
    moved = aside(True, near, *wave)
    for k in chunks[1]:
        moved += along(True, k, *wave)
    wave = moved + [theirs_down, theirs_kept_up, table]
    kept_theirs = (theirs_kept_gate, theirs_kept_up)
    mine, theirs = (w_gate, w_up, w_down), (theirs_gate, theirs_up, theirs_down)
    kept_mine = (saved_gate, saved_up)

    runs, came = {}, {True: [], False: []}
    sums = []
    half = len(chunks)
    for p in range(2 * half):
        backward, i = p < half, p % half
        moved = []
        if backward and i < last:
            for k in chunks[i + 1]:
                moved += aside(True, k, *wave)
            if i + 1 < last:
                for k in chunks[i + 2]:
                    moved += along(True, k, *wave)
        if p == half - 2:
            moved += aside(False, 0, *wave) + along(False, near, *wave)
            residual = relay(after(input_rows, *wave), 1, "T_y1")
            moved.append(residual)
        if p == half - 1:
            moved += aside(False, near, *wave)
        if 0 <= p - half + 1 < last:
            for k in chunks[p - half + 2]:
                moved += along(False, k, *wave)
        if 0 <= p - half < last:
            for k in chunks[p - half + 1]:
                moved += aside(False, k, *wave)
        for way, chunk_sums in sums:
            moved += send_sums(way, chunk_sums, *wave)
        sums = []
        if p:
            way, j = p <= half, (p - 1) % half
            own, sent = runs[p - 1]
            chunk_sums, arrived = chip_sums(
                way, chunks[j], own, sent, f"T_{names[way]}_s{j}", *wave
            )
            sums = [(way, chunk_sums)]
            moved.append(arrived)
        runs[p] = experts_on(backward, i, *wave)
        wave = moved + list(runs[p][1])
    def summed(values):
        total = values[0].astype(f32)
        for value in values[1:]:
            total = total + value.astype(f32)
        return total

    weighted = summed(came[True])
    saved_input = x_backward[0].astype(f32)
    scale_rows = inverse_rms(x_backward[0])
    inner = jnp.mean(weighted * saved_input, axis=-1, keepdims=True)
    d_input = (
        dy_backward[0].astype(f32)
        + scale_rows * weighted
        - saved_input * scale_rows * scale_rows * scale_rows * inner
    ).astype(bf16)
    next_backward = relay(d_input, -1, "T_b_y")

    send_sums(*sums[0], *wave)
    own, sent = runs[2 * half - 1]
    ahead = d_input
    for k, value in zip(chunks[last], sent):
        arrived = swap(after(value, *wave), 2, f"T_f_s{k}")
        send_sums(False, {k: after(chip_sum(False, k, own[k], arrived), ahead)})
        ahead, wave = came[False][-1], [arrived]
    next_forward = (summed(came[False]) + residual.astype(f32)).astype(bf16)
    return (next_forward[None], next_backward[None])


def solution(mesh):
    rows = P("section", "expert", None)
    weights = P("section", "expert", None, None)
    saved = P("section", "expert", None, None, None)
    placed = (
        rows, P("section", None), weights, weights, weights, rows, rows,
        rows, rows, rows, rows, saved, saved,
    )
    return jax.shard_map(
        shards, mesh=mesh, in_specs=placed, out_specs=(rows, rows), check_vma=False
    )
```

```python
import functools

import jax
import jax.numpy as jnp
from jax import lax
from jax.experimental import pallas as pl
from jax.experimental.pallas import tpu as pltpu
from jax.sharding import PartitionSpec as P

epsilon = 1e-06
f32 = jnp.float32
bf16 = jnp.bfloat16
LANES = 128
TILE = 256
OWN = bf16
VMEM_LIMIT = 56 * 1024 * 1024
PACK_VMEM_LIMIT = 56 * 1024 * 1024
TURNED = (((1,), (1,)), ((), ()))


def inverse_rms(values):
    widened = values.astype(f32)
    return lax.rsqrt(jnp.mean(widened * widened, axis=-1, keepdims=True) + epsilon)


def pack_kernel(experts, dy, x, gain, ids_b, gates_b, ids_f, gates_f, out_b, out_f):
    tokens, width = dy.shape
    wide = x[...].astype(f32)
    scale = lax.rsqrt(jnp.mean(wide * wide, axis=-1, keepdims=True) + epsilon)
    values = (dy[...], (wide * scale * gain[...]).astype(bf16))
    spread = (experts, out_b.shape[1] - width)
    row = lax.broadcasted_iota(jnp.int32, spread, 0)
    lane = lax.broadcasted_iota(jnp.int32, spread, 1)
    first = jnp.where(lane == row, 1.0, 0.0).astype(bf16)
    second = jnp.where(lane == row + experts, 1.0, 0.0).astype(bf16)
    expert = lax.broadcasted_iota(jnp.int32, (experts, tokens), 0)
    turned = (((0,), (0,)), ((), ()))
    for i, (ids, gates, out) in enumerate(((ids_b, gates_b, out_b), (ids_f, gates_f, out_f))):
        dense = jnp.zeros((experts, tokens), f32)
        for k in range(ids.shape[0]):
            dense = dense + jnp.where(expert == ids[k : k + 1, :], gates[k : k + 1, :], 0.0)
        high = dense.astype(bf16)
        low = (dense - high.astype(f32)).astype(bf16)
        columns = lax.dot_general(high, first, turned, preferred_element_type=f32)
        columns += lax.dot_general(low, second, turned, preferred_element_type=f32)
        out[:, :width] = values[i]
        out[:, width:] = columns.astype(bf16)


def pack(experts, dy, x, gain, ids_b, gates_b, ids_f, gates_f):
    tokens, width = dy.shape
    columns = -(-2 * experts // LANES) * LANES
    vmem = pl.BlockSpec(memory_space=pltpu.VMEM)
    one = jax.ShapeDtypeStruct((tokens, width + columns), bf16)
    return pl.pallas_call(
        functools.partial(pack_kernel, experts),
        out_shape=[one, one],
        in_specs=[vmem] * 7,
        out_specs=[vmem] * 2,
        compiler_params=pltpu.CompilerParams(vmem_limit_bytes=PACK_VMEM_LIMIT),
        name="pack",
    )(dy, x, gain, ids_b.T, gates_b.T, ids_f.T, gates_f.T)


def experts_kernel(backward, experts, tokens, capacity, chunk, apart, starts, table, *refs):
    count = len(starts)
    rows, refs = refs[:count], refs[count:]
    weights, refs = (refs[:3], refs[3:6]), refs[6:]
    if backward:
        kept, gain, refs = (refs[:2], refs[2:4]), refs[4], refs[5:]
    outs, refs = refs[: count // 2], refs[count // 2 :]
    sent, refs = (refs[: count // 2], refs[count // 2 :]) if apart else (refs[:1], refs[1:])
    gathered, columns_of, hidden, gates_ups, downs, sems = refs[:6]
    amount = count * tokens
    width = gathered.shape[1]
    inner = hidden.shape[1] // (4 if backward else 2)
    spaced = -(-capacity // 16) * 16
    slots = count * spaced

    copies = []

    def fetch(source, target):
        copies.append(pltpu.make_async_copy(source, target, sems.at[len(copies)]))
        copies[-1].start()
        return copies[-1]

    def fetch_first(e):
        if not backward:
            return [fetch(weights[e][j].at[0, 0], gates_ups.at[e, j]) for j in range(2)]
        group = [fetch(weights[e][2].at[0, 0], downs.at[e])]
        for i in range(count):
            block = table[chunk, 2 + i]
            for j in range(2):
                to = refs[6].at[e, j, i * spaced : i * spaced + capacity, :]
                group.append(fetch(kept[e][j].at[0, 0, block], to))
        return group

    def fetch_second(e):
        if not backward:
            return [fetch(weights[e][2].at[0, 0], downs.at[e])]
        return [fetch(weights[e][j].at[0, 0], gates_ups.at[e, j]) for j in range(2)]

    if backward and spaced != capacity:
        refs[6][...] = jnp.zeros_like(refs[6])
    group = []
    for i in range(count):
        here = slice(i * tokens, (i + 1) * tokens)
        source = slice(starts[i], starts[i] + tokens)
        group.append(fetch(rows[i].at[source, :width], gathered.at[here, :]))
        group.append(fetch(rows[i].at[source, width:], columns_of.at[here, :]))
    groups = [group, fetch_first(0), fetch_first(1)]
    for copy in groups[0]:
        copy.wait()

    columns = columns_of[...].astype(f32)
    lane = lax.broadcasted_iota(jnp.int32, columns.shape, 1)
    if backward:
        row = lax.broadcasted_iota(jnp.int32, (amount, amount), 0)
        column = lax.broadcasted_iota(jnp.int32, (amount, amount), 1)
        below = column < row
        placed_row = lax.broadcasted_iota(jnp.int32, (amount, slots), 0)
        base = jnp.zeros((amount, slots), jnp.int32)
        for i in range(1, count):
            below = below & ((row < i * tokens) | (column >= i * tokens))
            base = jnp.where(placed_row >= i * tokens, i * spaced, base)
        below = jnp.where(below, 1.0, 0.0).astype(bf16)
        slot_lane = lax.broadcasted_iota(jnp.int32, (amount, slots), 1)

    for e in range(2):
        expert = table[chunk, e]
        chosen = (lane == expert) | (lane == expert + experts)
        gate = jnp.sum(jnp.where(chosen, columns, 0.0), axis=1, keepdims=True)
        if backward:
            routed = jnp.broadcast_to(jnp.where(gate > 0.0, 1.0, 0.0), (amount, slots))
            before = jnp.dot(below, routed.astype(bf16), preferred_element_type=f32)
            target = before.astype(jnp.int32) + base
            place = jnp.where((slot_lane == target) & (routed > 0.0), 1.0, 0.0).astype(bf16)
        for copy in groups[1 + e]:
            copy.wait()
        groups.append(fetch_second(e))
        value = gathered[...]
        if not backward:
            gate_pre = jnp.dot(value, gates_ups[e, 0], preferred_element_type=f32)
            up_pre = jnp.dot(value, gates_ups[e, 1], preferred_element_type=f32)
            act = gate_pre * jax.nn.sigmoid(gate_pre) * (up_pre * gate)
            hidden[:, e * inner : (e + 1) * inner] = act.astype(bf16)
            continue
        d_act = gate * lax.dot_general(value, downs[e], TURNED, preferred_element_type=f32)
        g = jnp.dot(place, refs[6][e, 0], preferred_element_type=f32)
        u = jnp.dot(place, refs[6][e, 1], preferred_element_type=f32)
        q = jax.nn.sigmoid(g)
        at = 2 * e * inner
        hidden[:, at : at + inner] = (d_act * u * q * (1.0 + g * (1.0 - q))).astype(bf16)
        hidden[:, at + inner : at + 2 * inner] = (d_act * g * q).astype(bf16)

    total = None
    for e in range(2):
        for copy in groups[3 + e]:
            copy.wait()
        if backward:
            for j in range(2):
                left = hidden[:, (2 * e + j) * inner : (2 * e + j + 1) * inner]
                term = lax.dot_general(left, gates_ups[e, j], TURNED, preferred_element_type=f32)
                total = term if total is None else total + term
        else:
            left = hidden[:, e * inner : (e + 1) * inner]
            term = jnp.dot(left, downs[e], preferred_element_type=f32)
            total = term if total is None else total + term
    if backward:
        total = total * gain[...]
    for i in range(count):
        piece = total[i * tokens : (i + 1) * tokens, :]
        if i % 2 == 0:
            outs[i // 2][...] = piece.astype(outs[i // 2].dtype)
        else:
            at = 0 if apart else i // 2 * tokens
            sent[i // 2 if apart else 0][at : at + tokens, :] = piece.astype(bf16)


def run_experts(backward, experts, tokens, chunk, apart, table, rows, mine, theirs, kept_mine, kept_theirs, gain):
    count = len(rows)
    starts = [start for _, start in rows]
    rows = [array for array, _ in rows]
    width, inner = mine[0].shape[2:]
    capacity = kept_mine[0].shape[3]
    spaced = -(-capacity // 16) * 16
    vmem, anywhere = pl.BlockSpec(memory_space=pltpu.VMEM), pl.BlockSpec(memory_space=pl.ANY)
    operands = list(rows) + list(mine) + list(theirs)
    copies = 2 * count + 6
    scratch = [
        pltpu.VMEM((count * tokens, width), bf16),
        pltpu.VMEM((count * tokens, rows[0].shape[1] - width), bf16),
        pltpu.VMEM((count * tokens, (4 if backward else 2) * inner), bf16),
        pltpu.VMEM((2, 2, width, inner), bf16),
        pltpu.VMEM((2, inner, width), bf16),
    ]
    in_specs = [pl.BlockSpec(memory_space=pltpu.SMEM)] + [anywhere] * len(operands)
    if backward:
        operands += list(kept_mine) + list(kept_theirs) + [gain]
        in_specs += [anywhere] * 4 + [vmem]
        copies += 4 * count
    scratch.append(pltpu.SemaphoreType.DMA((copies,)))
    if backward:
        scratch.append(pltpu.VMEM((2, 2, count * spaced, inner), bf16))
    out_shape = [jax.ShapeDtypeStruct((tokens, width), OWN)] * (count // 2)
    if apart:
        out_shape += [jax.ShapeDtypeStruct((tokens, width), bf16)] * (count // 2)
    else:
        out_shape += [jax.ShapeDtypeStruct((count // 2 * tokens, width), bf16)]
    return pl.pallas_call(
        functools.partial(
            experts_kernel, backward, experts, tokens, capacity, chunk, apart, starts
        ),
        out_shape=out_shape,
        in_specs=in_specs,
        out_specs=[vmem] * len(out_shape),
        scratch_shapes=scratch,
        compiler_params=pltpu.CompilerParams(vmem_limit_bytes=VMEM_LIMIT),
        cost_estimate=pl.CostEstimate(
            flops=12 * count * tokens * width * inner,
            bytes_accessed=12 * width * inner,
            transcendentals=0,
        ),
        name="experts_backward" if backward else "experts_forward",
    )(table, *operands)


def shards(
    x_forward,
    norm_gain,
    w_gate,
    w_up,
    w_down,
    ids_forward,
    gates_forward,
    x_backward,
    dy_backward,
    ids_backward,
    gates_backward,
    saved_gate,
    saved_up,
):
    experts = lax.axis_size("expert")
    sections = lax.axis_size("section")
    line = experts // 4
    me = lax.axis_index("expert")
    a, b, c = me // 4, (me // 2) % 2, me % 2

    def swap(value, bit, label):
        with jax.named_scope(label):
            return lax.ppermute(value, "expert", [(i, i ^ bit) for i in range(experts)])

    def shift(value, steps, label):
        with jax.named_scope(label):
            return lax.ppermute(
                value, "expert", [(i, (i + 4 * steps) % experts) for i in range(experts)]
            )

    def relay(value, section_steps, label, steps=0):
        pairs = []
        for s in range(sections):
            for i in range(experts):
                target = ((s + section_steps) % sections) * experts + (i + 4 * steps) % experts
                pairs.append((s * experts + i, target))
        with jax.named_scope(label):
            return lax.ppermute(value, ("section", "expert"), pairs)

    order = [0, 1]
    for k in range(2, line // 2 + 1):
        order += [k, line + 1 - k]
    chunks = [order[i : i + 2] for i in range(0, line, 2)]
    last = len(chunks) - 1

    def after(value, *others):
        return lax.optimization_barrier((value,) + others)[0]

    def farther(held, k, label):
        if 2 * k <= line:
            return shift(held[k - 1], 1, f"T_{label}_z{k}")
        return shift(held[(k + 1) % line], -1, f"T_{label}_z{k}")

    def block_of(k, other):
        return (((a - k) % line) * 2 + (b ^ other)) * 2 + c

    def scalars_of(chunk):
        blocks = [block_of(k, o) for k in chunk for o in (0, 1)]
        return jnp.stack([me, me ^ 1] + blocks).astype(jnp.int32)

    gain = norm_gain
    input_rows = x_forward[0]
    tokens = input_rows.shape[0]
    table = jnp.stack([scalars_of(chunk) for chunk in chunks])
    packed = pack(
        experts, dy_backward[0], input_rows, gain,
        ids_backward[0], gates_backward[0], ids_forward[0], gates_forward[0],
    )
    held = {True: {0: packed[0]}, False: {0: packed[1]}}
    across = {True: {}, False: {}}
    names = {True: "b", False: "f"}

    def along(backward, k, *earlier):
        ready = {j: after(v, *earlier) for j, v in held[backward].items()}
        held[backward][k] = farther(ready, k, names[backward])
        return [held[backward][k]]

    def aside(backward, k, hop, *earlier):
        known, name = across[backward], names[backward]
        if hop:
            value = after(known[(k - hop) % line], *earlier)
            known[k] = shift(value, hop, f"T_{name}_w{k}")
        else:
            known[k] = swap(after(held[backward][k], *earlier), 2, f"T_{name}_x{k}")
        return [known[k]]

    def experts_on(backward, chunk, *earlier):
        apart = not backward and chunk == chunks[last]
        rows = [(r, 0) for k in chunk for r in (held[backward][k], across[backward][k])]
        out = run_experts(
            backward, experts, tokens, chunks.index(chunk), apart,
            after(table, *earlier), rows, mine, theirs, kept_mine, kept_theirs, gain,
        )
        return dict(zip(chunk, out)), out[len(chunk) :]

    def chip_sum(backward, k, own, piece):
        total = own.astype(f32) + piece.astype(f32)
        return total if k == 0 else total.astype(bf16)

    def chip_sums(backward, chunk, own, sent, label, *earlier):
        came = swap(after(sent[0], *earlier), 2, label)
        pieces = {k: came[i * tokens : (i + 1) * tokens] for i, k in enumerate(chunk)}
        return {k: chip_sum(backward, k, own[k], piece) for k, piece in pieces.items()}, came

    def send_sums(backward, sums, *earlier):
        moved = []
        for k, value in sums.items():
            label, value = f"T_{names[backward]}_r{k}", after(value, *earlier)
            if not backward:
                moved.append(relay(value, 1, label, -k))
            elif k:
                moved.append(shift(value, -k, label))
            else:
                came[True].append(value)
        came[backward].extend(moved)
        return moved

    near = chunks[0][1]
    wave = along(True, near) + aside(True, 0, 0)
    theirs_gate = swap(after(w_gate, packed[0]), 1, "T_wg")
    theirs_kept_gate = swap(after(saved_gate, packed[0]), 1, "T_sg")
    theirs_kept_up = swap(after(saved_up, packed[0]), 1, "T_su")
    wave += [theirs_gate, theirs_kept_gate, theirs_kept_up]
    table = after(table, *wave)
    theirs_up = swap(after(w_up, *wave), 1, "T_wu")
    theirs_down = swap(after(w_down, *wave), 1, "T_wd")
    moved = aside(True, near, 0, *wave)
    for k in chunks[1]:
        moved += along(True, k, *wave)
    wave = moved + [theirs_up, theirs_down, table]
    kept_theirs = (theirs_kept_gate, theirs_kept_up)
    mine, theirs = (w_gate, w_up, w_down), (theirs_gate, theirs_up, theirs_down)
    kept_mine = (saved_gate, saved_up)

    def summed(values):
        total = values[0].astype(f32)
        for value in values[1:]:
            total = total + value.astype(f32)
        return total

    def end_backward(*earlier):
        weighted = summed([after(value, *earlier) for value in came[True]])
        saved_input = x_backward[0].astype(f32)
        scale_rows = inverse_rms(x_backward[0])
        inner = jnp.mean(weighted * saved_input, axis=-1, keepdims=True)
        d_input = (
            dy_backward[0].astype(f32)
            + scale_rows * weighted
            - saved_input * scale_rows * scale_rows * scale_rows * inner
        ).astype(bf16)
        return d_input

    half = len(chunks)
    works = [(True, chunk) for chunk in chunks] + [(False, chunk) for chunk in chunks]
    runs, came, sums = [], {True: [], False: []}, {}
    for p, (backward, chunk) in enumerate(works):
        moved = []
        if p < last:
            right, left = chunks[p + 1]
            moved += aside(True, right, 0, *wave) + aside(True, left, -1, *wave)
            if p + 1 < last:
                for k in chunks[p + 2]:
                    moved += along(True, k, *wave)
        if p == half - 2:
            moved += aside(False, 0, 0, *wave) + along(False, near, *wave)
            residual = relay(after(input_rows, *wave), 1, "T_y1")
            moved.append(residual)
        if p == half - 1:
            moved += aside(False, near, 0, *wave)
        if 0 < p - half + 2 <= last:
            for k in chunks[p - half + 2]:
                moved += along(False, k, *wave)
        if 0 < p - half + 1 <= last:
            right, left = chunks[p - half + 1]
            moved += aside(False, right, 0, *wave) + aside(False, left, -1, *wave)
        if p == half + 2:
            near_sums = sums[half]
        elif p >= 2:
            moved += send_sums(works[p - 2][0], sums[p - 2], *wave)
        if p:
            way, before = works[p - 1]
            own, sent = runs[p - 1]
            label = f"T_{names[way]}_s{before[0]}"
            sums[p - 1], arrived = chip_sums(way, before, own, sent, label, *wave)
            moved.append(arrived)
        runs.append(experts_on(backward, chunk, *wave))
        wave = moved + list(runs[p][1])
    own, sent = runs[-1]
    d_input = end_backward(*wave)
    next_backward = relay(d_input, -1, "T_b_y")
    def end_near(*earlier):
        part = shift(after(near_sums[near], *earlier), -near, "T_f_near")
        return (near_sums[0] + part.astype(f32)).astype(bf16)

    if half > 2:
        send_sums(False, sums[len(works) - 2], *wave)
        joined = end_near(*wave)
    else:
        near_sums = sums[len(works) - 2]
        joined = end_near(*wave)
    came[False].append(relay(joined, 1, "T_f_joined"))
    before, ahead = wave, d_input
    for k, value in zip(chunks[last], sent):
        arrived = swap(after(value, *before), 2, f"T_f_s{k}")
        final = chip_sum(False, k, own[k], arrived)
        send_sums(False, {k: after(final, ahead)})
        before, ahead = [arrived], joined
    next_forward = (summed(came[False]) + residual.astype(f32)).astype(bf16)
    return (next_forward[None], next_backward[None])


def solution(mesh):
    rows = P("section", "expert", None)
    weights = P("section", "expert", None, None)
    saved = P("section", "expert", None, None, None)
    placed = (
        rows, P("section", None), weights, weights, weights, rows, rows,
        rows, rows, rows, rows, saved, saved,
    )
    return jax.shard_map(
        shards, mesh=mesh, in_specs=placed, out_specs=(rows, rows), check_vma=False
    )
```

```python
import functools

import jax
import jax.numpy as jnp
from jax import lax
from jax.experimental import pallas as pl
from jax.experimental.pallas import tpu as pltpu
from jax.sharding import PartitionSpec as P

epsilon = 1e-06
f32 = jnp.float32
bf16 = jnp.bfloat16
LANES = 128
TILE = 256
OWN = bf16
VMEM_LIMIT = 56 * 1024 * 1024
PACK_VMEM_LIMIT = 56 * 1024 * 1024
TURNED = (((1,), (1,)), ((), ()))


def inverse_rms(values):
    widened = values.astype(f32)
    return lax.rsqrt(jnp.mean(widened * widened, axis=-1, keepdims=True) + epsilon)


def pack_kernel(experts, dy, x, gain, ids_b, gates_b, ids_f, gates_f, out_b, out_f):
    tokens, width = dy.shape
    wide = x[...].astype(f32)
    scale = lax.rsqrt(jnp.mean(wide * wide, axis=-1, keepdims=True) + epsilon)
    values = (dy[...], (wide * scale * gain[...]).astype(bf16))
    spread = (experts, out_b.shape[1] - width)
    row = lax.broadcasted_iota(jnp.int32, spread, 0)
    lane = lax.broadcasted_iota(jnp.int32, spread, 1)
    first = jnp.where(lane == row, 1.0, 0.0).astype(bf16)
    second = jnp.where(lane == row + experts, 1.0, 0.0).astype(bf16)
    expert = lax.broadcasted_iota(jnp.int32, (experts, tokens), 0)
    turned = (((0,), (0,)), ((), ()))
    for i, (ids, gates, out) in enumerate(((ids_b, gates_b, out_b), (ids_f, gates_f, out_f))):
        dense = jnp.zeros((experts, tokens), f32)
        for k in range(ids.shape[0]):
            dense = dense + jnp.where(expert == ids[k : k + 1, :], gates[k : k + 1, :], 0.0)
        high = dense.astype(bf16)
        low = (dense - high.astype(f32)).astype(bf16)
        columns = lax.dot_general(high, first, turned, preferred_element_type=f32)
        columns += lax.dot_general(low, second, turned, preferred_element_type=f32)
        out[:, :width] = values[i]
        out[:, width:] = columns.astype(bf16)


def pack(experts, dy, x, gain, ids_b, gates_b, ids_f, gates_f):
    tokens, width = dy.shape
    columns = -(-2 * experts // LANES) * LANES
    vmem = pl.BlockSpec(memory_space=pltpu.VMEM)
    one = jax.ShapeDtypeStruct((tokens, width + columns), bf16)
    return pl.pallas_call(
        functools.partial(pack_kernel, experts),
        out_shape=[one, one],
        in_specs=[vmem] * 7,
        out_specs=[vmem] * 2,
        compiler_params=pltpu.CompilerParams(vmem_limit_bytes=PACK_VMEM_LIMIT),
        name="pack",
    )(dy, x, gain, ids_b.T, gates_b.T, ids_f.T, gates_f.T)


def experts_kernel(backward, experts, tokens, capacity, chunk, apart, starts, table, *refs):
    count = len(starts)
    rows, refs = refs[:count], refs[count:]
    weights, refs = (refs[:3], refs[3:6]), refs[6:]
    if backward:
        kept, gain, refs = (refs[:2], refs[2:4]), refs[4], refs[5:]
    outs, refs = refs[: count // 2], refs[count // 2 :]
    sent, refs = (refs[: count // 2], refs[count // 2 :]) if apart else (refs[:1], refs[1:])
    gathered, columns_of, hidden, gates_ups, downs, sems = refs[:6]
    amount = count * tokens
    width = gathered.shape[1]
    inner = hidden.shape[1] // (4 if backward else 2)
    spaced = -(-capacity // 16) * 16
    slots = count * spaced

    copies = []

    def fetch(source, target):
        copies.append(pltpu.make_async_copy(source, target, sems.at[len(copies)]))
        copies[-1].start()
        return copies[-1]

    def fetch_first(e):
        if not backward:
            return [fetch(weights[e][j].at[0, 0], gates_ups.at[e, j]) for j in range(2)]
        group = [fetch(weights[e][2].at[0, 0], downs.at[e])]
        for i in range(count):
            block = table[chunk, 2 + i]
            for j in range(2):
                to = refs[6].at[e, j, i * spaced : i * spaced + capacity, :]
                group.append(fetch(kept[e][j].at[0, 0, block], to))
        return group

    def fetch_second(e):
        if not backward:
            return [fetch(weights[e][2].at[0, 0], downs.at[e])]
        return [fetch(weights[e][j].at[0, 0], gates_ups.at[e, j]) for j in range(2)]

    if backward and spaced != capacity:
        refs[6][...] = jnp.zeros_like(refs[6])
    group = []
    for i in range(count):
        here = slice(i * tokens, (i + 1) * tokens)
        source = slice(starts[i], starts[i] + tokens)
        group.append(fetch(rows[i].at[source, :width], gathered.at[here, :]))
        group.append(fetch(rows[i].at[source, width:], columns_of.at[here, :]))
    groups = [group, fetch_first(0), fetch_first(1)]
    for copy in groups[0]:
        copy.wait()

    columns = columns_of[...].astype(f32)
    lane = lax.broadcasted_iota(jnp.int32, columns.shape, 1)
    if backward:
        row = lax.broadcasted_iota(jnp.int32, (amount, amount), 0)
        column = lax.broadcasted_iota(jnp.int32, (amount, amount), 1)
        below = column < row
        placed_row = lax.broadcasted_iota(jnp.int32, (amount, slots), 0)
        base = jnp.zeros((amount, slots), jnp.int32)
        for i in range(1, count):
            below = below & ((row < i * tokens) | (column >= i * tokens))
            base = jnp.where(placed_row >= i * tokens, i * spaced, base)
        below = jnp.where(below, 1.0, 0.0).astype(bf16)
        slot_lane = lax.broadcasted_iota(jnp.int32, (amount, slots), 1)

    for e in range(2):
        expert = table[chunk, e]
        chosen = (lane == expert) | (lane == expert + experts)
        gate = jnp.sum(jnp.where(chosen, columns, 0.0), axis=1, keepdims=True)
        if backward:
            routed = jnp.broadcast_to(jnp.where(gate > 0.0, 1.0, 0.0), (amount, slots))
            before = jnp.dot(below, routed.astype(bf16), preferred_element_type=f32)
            target = before.astype(jnp.int32) + base
            place = jnp.where((slot_lane == target) & (routed > 0.0), 1.0, 0.0).astype(bf16)
        for copy in groups[1 + e]:
            copy.wait()
        groups.append(fetch_second(e))
        value = gathered[...]
        if not backward:
            gate_pre = jnp.dot(value, gates_ups[e, 0], preferred_element_type=f32)
            up_pre = jnp.dot(value, gates_ups[e, 1], preferred_element_type=f32)
            act = gate_pre * jax.nn.sigmoid(gate_pre) * (up_pre * gate)
            hidden[:, e * inner : (e + 1) * inner] = act.astype(bf16)
            continue
        d_act = gate * lax.dot_general(value, downs[e], TURNED, preferred_element_type=f32)
        g = jnp.dot(place, refs[6][e, 0], preferred_element_type=f32)
        u = jnp.dot(place, refs[6][e, 1], preferred_element_type=f32)
        q = jax.nn.sigmoid(g)
        at = 2 * e * inner
        hidden[:, at : at + inner] = (d_act * u * q * (1.0 + g * (1.0 - q))).astype(bf16)
        hidden[:, at + inner : at + 2 * inner] = (d_act * g * q).astype(bf16)

    total = None
    for e in range(2):
        for copy in groups[3 + e]:
            copy.wait()
        if backward:
            for j in range(2):
                left = hidden[:, (2 * e + j) * inner : (2 * e + j + 1) * inner]
                term = lax.dot_general(left, gates_ups[e, j], TURNED, preferred_element_type=f32)
                total = term if total is None else total + term
        else:
            left = hidden[:, e * inner : (e + 1) * inner]
            term = jnp.dot(left, downs[e], preferred_element_type=f32)
            total = term if total is None else total + term
    if backward:
        total = total * gain[...]
    for i in range(count):
        piece = total[i * tokens : (i + 1) * tokens, :]
        if i % 2 == 0:
            outs[i // 2][...] = piece.astype(outs[i // 2].dtype)
        else:
            at = 0 if apart else i // 2 * tokens
            sent[i // 2 if apart else 0][at : at + tokens, :] = piece.astype(bf16)


def run_experts(backward, experts, tokens, chunk, apart, table, rows, mine, theirs, kept_mine, kept_theirs, gain):
    count = len(rows)
    starts = [start for _, start in rows]
    rows = [array for array, _ in rows]
    width, inner = mine[0].shape[2:]
    capacity = kept_mine[0].shape[3]
    spaced = -(-capacity // 16) * 16
    vmem, anywhere = pl.BlockSpec(memory_space=pltpu.VMEM), pl.BlockSpec(memory_space=pl.ANY)
    operands = list(rows) + list(mine) + list(theirs)
    copies = 2 * count + 6
    scratch = [
        pltpu.VMEM((count * tokens, width), bf16),
        pltpu.VMEM((count * tokens, rows[0].shape[1] - width), bf16),
        pltpu.VMEM((count * tokens, (4 if backward else 2) * inner), bf16),
        pltpu.VMEM((2, 2, width, inner), bf16),
        pltpu.VMEM((2, inner, width), bf16),
    ]
    in_specs = [pl.BlockSpec(memory_space=pltpu.SMEM)] + [anywhere] * len(operands)
    if backward:
        operands += list(kept_mine) + list(kept_theirs) + [gain]
        in_specs += [anywhere] * 4 + [vmem]
        copies += 4 * count
    scratch.append(pltpu.SemaphoreType.DMA((copies,)))
    if backward:
        scratch.append(pltpu.VMEM((2, 2, count * spaced, inner), bf16))
    out_shape = [jax.ShapeDtypeStruct((tokens, width), OWN)] * (count // 2)
    if apart:
        out_shape += [jax.ShapeDtypeStruct((tokens, width), bf16)] * (count // 2)
    else:
        out_shape += [jax.ShapeDtypeStruct((count // 2 * tokens, width), bf16)]
    return pl.pallas_call(
        functools.partial(
            experts_kernel, backward, experts, tokens, capacity, chunk, apart, starts
        ),
        out_shape=out_shape,
        in_specs=in_specs,
        out_specs=[vmem] * len(out_shape),
        scratch_shapes=scratch,
        compiler_params=pltpu.CompilerParams(vmem_limit_bytes=VMEM_LIMIT),
        cost_estimate=pl.CostEstimate(
            flops=12 * count * tokens * width * inner,
            bytes_accessed=12 * width * inner,
            transcendentals=0,
        ),
        name="experts_backward" if backward else "experts_forward",
    )(table, *operands)


def place_kernel(arrived, out):
    out[...] = arrived[...]


def placed_early(arrived):
    return pl.pallas_call(
        place_kernel, out_shape=jax.ShapeDtypeStruct(arrived.shape, arrived.dtype), name="place"
    )(arrived)


def shards(
    x_forward,
    norm_gain,
    w_gate,
    w_up,
    w_down,
    ids_forward,
    gates_forward,
    x_backward,
    dy_backward,
    ids_backward,
    gates_backward,
    saved_gate,
    saved_up,
):
    experts = lax.axis_size("expert")
    sections = lax.axis_size("section")
    line = experts // 4
    me = lax.axis_index("expert")
    a, b, c = me // 4, (me // 2) % 2, me % 2

    def swap(value, bit, label):
        with jax.named_scope(label):
            return lax.ppermute(value, "expert", [(i, i ^ bit) for i in range(experts)])

    def shift(value, steps, label):
        with jax.named_scope(label):
            return lax.ppermute(
                value, "expert", [(i, (i + 4 * steps) % experts) for i in range(experts)]
            )

    def relay(value, section_steps, label, steps=0):
        pairs = []
        for s in range(sections):
            for i in range(experts):
                target = ((s + section_steps) % sections) * experts + (i + 4 * steps) % experts
                pairs.append((s * experts + i, target))
        with jax.named_scope(label):
            return lax.ppermute(value, ("section", "expert"), pairs)

    order = [0, 1]
    for k in range(2, line // 2 + 1):
        order += [k, line + 1 - k]
    chunks = [order[i : i + 2] for i in range(0, line, 2)]
    last = len(chunks) - 1

    def after(value, *others):
        return lax.optimization_barrier((value,) + others)[0]

    def farther(held, k, label):
        if 2 * k <= line:
            return shift(held[k - 1], 1, f"T_{label}_z{k}")
        return shift(held[(k + 1) % line], -1, f"T_{label}_z{k}")

    def block_of(k, other):
        return (((a - k) % line) * 2 + (b ^ other)) * 2 + c

    def scalars_of(chunk):
        blocks = [block_of(k, o) for k in chunk for o in (0, 1)]
        return jnp.stack([me, me ^ 1] + blocks).astype(jnp.int32)

    gain = norm_gain
    input_rows = x_forward[0]
    tokens = input_rows.shape[0]
    table = jnp.stack([scalars_of(chunk) for chunk in chunks])
    packed = pack(
        experts, dy_backward[0], input_rows, gain,
        ids_backward[0], gates_backward[0], ids_forward[0], gates_forward[0],
    )
    held = {True: {0: packed[0]}, False: {0: packed[1]}}
    across = {True: {}, False: {}}
    names = {True: "b", False: "f"}

    def along(backward, k, *earlier):
        ready = {j: after(v, *earlier) for j, v in held[backward].items()}
        held[backward][k] = farther(ready, k, names[backward])
        return [held[backward][k]]

    def aside(backward, k, hop, *earlier):
        known, name = across[backward], names[backward]
        if hop:
            value = after(known[(k - hop) % line], *earlier)
            known[k] = shift(value, hop, f"T_{name}_w{k}")
        else:
            known[k] = swap(after(held[backward][k], *earlier), 2, f"T_{name}_x{k}")
        return [known[k]]

    def experts_on(backward, chunk, *earlier):
        apart = not backward and chunk == chunks[last]
        rows = [(r, 0) for k in chunk for r in (held[backward][k], across[backward][k])]
        out = run_experts(
            backward, experts, tokens, chunks.index(chunk), apart,
            after(table, *earlier), rows, mine, theirs, kept_mine, kept_theirs, gain,
        )
        return dict(zip(chunk, out)), out[len(chunk) :]

    def chip_sum(backward, k, own, piece):
        total = own.astype(f32) + piece.astype(f32)
        return total if k == 0 else total.astype(bf16)

    def chip_sums(backward, chunk, own, sent, label, *earlier):
        came = swap(after(sent[0], *earlier), 2, label)
        pieces = {k: came[i * tokens : (i + 1) * tokens] for i, k in enumerate(chunk)}
        return {k: chip_sum(backward, k, own[k], piece) for k, piece in pieces.items()}, came

    def send_sums(backward, sums, *earlier):
        moved = []
        for k, value in sums.items():
            label, value = f"T_{names[backward]}_r{k}", after(value, *earlier)
            if not backward:
                moved.append(relay(value, 1, label, -k))
            elif k:
                moved.append(shift(value, -k, label))
            else:
                came[True].append(value)
        came[backward].extend(moved)
        return moved

    near = chunks[0][1]
    wave = along(True, near) + aside(True, 0, 0)
    theirs_gate = swap(after(w_gate, packed[0]), 1, "T_wg")
    theirs_kept_gate = swap(after(saved_gate, packed[0]), 1, "T_sg")
    theirs_kept_up = swap(after(saved_up, packed[0]), 1, "T_su")
    wave += [theirs_gate, theirs_kept_gate, theirs_kept_up]
    table = after(table, *wave)
    theirs_up = swap(after(w_up, *wave), 1, "T_wu")
    theirs_down = swap(after(w_down, *wave), 1, "T_wd")
    moved = aside(True, near, 0, *wave)
    for k in chunks[1]:
        moved += along(True, k, *wave)
    wave = moved + [theirs_up, theirs_down, table]
    kept_theirs = (theirs_kept_gate, theirs_kept_up)
    mine, theirs = (w_gate, w_up, w_down), (theirs_gate, theirs_up, theirs_down)
    kept_mine = (saved_gate, saved_up)

    def summed(values):
        total = values[0].astype(f32)
        for value in values[1:]:
            total = total + value.astype(f32)
        return total

    def end_backward(*earlier):
        weighted = summed([after(value, *earlier) for value in came[True]])
        saved_input = x_backward[0].astype(f32)
        scale_rows = inverse_rms(x_backward[0])
        inner = jnp.mean(weighted * saved_input, axis=-1, keepdims=True)
        d_input = (
            dy_backward[0].astype(f32)
            + scale_rows * weighted
            - saved_input * scale_rows * scale_rows * scale_rows * inner
        ).astype(bf16)
        return d_input

    half = len(chunks)
    works = [(True, chunk) for chunk in chunks] + [(False, chunk) for chunk in chunks]
    runs, came, sums = [], {True: [], False: []}, {}
    for p, (backward, chunk) in enumerate(works):
        moved = []
        if p < last:
            right, left = chunks[p + 1]
            moved += aside(True, right, 0, *wave) + aside(True, left, -1, *wave)
            if p + 1 < last:
                for k in chunks[p + 2]:
                    moved += along(True, k, *wave)
        if p == half - 2:
            moved += aside(False, 0, 0, *wave) + along(False, near, *wave)
            residual = relay(after(input_rows, *wave), 1, "T_y1")
            moved.append(residual)
        if p == half - 1:
            moved += aside(False, near, 0, *wave)
        if 0 < p - half + 2 <= last:
            for k in chunks[p - half + 2]:
                moved += along(False, k, *wave)
        if 0 < p - half + 1 <= last:
            right, left = chunks[p - half + 1]
            moved += aside(False, right, 0, *wave) + aside(False, left, -1, *wave)
        if p == half + 2:
            near_sums = sums[half]
        elif p >= 2:
            moved += send_sums(works[p - 2][0], sums[p - 2], *wave)
        if p:
            way, before = works[p - 1]
            own, sent = runs[p - 1]
            label = f"T_{names[way]}_s{before[0]}"
            sums[p - 1], arrived = chip_sums(way, before, own, sent, label, *wave)
            moved.append(arrived)
        runs.append(experts_on(backward, chunk, *wave))
        wave = moved + list(runs[p][1])
    own, sent = runs[-1]
    d_input = end_backward(*wave)
    next_backward = relay(d_input, -1, "T_b_y")
    def end_near(*earlier):
        part = shift(after(near_sums[near], *earlier), -near, "T_f_near")
        return (near_sums[0] + part.astype(f32)).astype(bf16)

    if half > 2:
        send_sums(False, sums[len(works) - 2], *wave)
        joined = end_near(*wave)
    else:
        near_sums = sums[len(works) - 2]
        joined = end_near(*wave)
    came[False].append(relay(joined, 1, "T_f_joined"))
    before, ahead = wave, d_input
    for k, value in zip(chunks[last], sent):
        arrived = swap(after(value, *before), 2, f"T_f_s{k}")
        final = chip_sum(False, k, own[k], arrived)
        send_sums(False, {k: after(final, ahead)})
        before, ahead = [arrived], joined
    next_backward = placed_early(next_backward)
    came[False] = [after(value, next_backward) for value in came[False]]
    next_forward = (summed(came[False]) + residual.astype(f32)).astype(bf16)
    return (next_forward[None], next_backward[None])


def solution(mesh):
    rows = P("section", "expert", None)
    weights = P("section", "expert", None, None)
    saved = P("section", "expert", None, None, None)
    placed = (
        rows, P("section", None), weights, weights, weights, rows, rows,
        rows, rows, rows, rows, saved, saved,
    )
    return jax.shard_map(
        shards, mesh=mesh, in_specs=placed, out_specs=(rows, rows), check_vma=False
    )
```
